256 devices in a mesh: req: 128 (over z, y, x_hi, core), kv: 2 (over x_lo).
Axes of the slice: x: 4 (x_hi: 2, x_lo: 2; x = x_hi * 2 + x_lo), y: 4, z: 8, core: 2. Of those that a mesh axis runs over, the one named last changes fastest.
Arguments:
- hidden: bfloat16 [1024, 2048], P('req'), may hold values from -1.796875 to 1.796875
- queries: bfloat16 [1024, 2048], P('req', 'kv'), may hold values from -30 to 30
- fresh_key_value: bfloat16 [1024, 4, 256], P('req', 'kv'), may hold values from -6 to 6
- kv_pool: bfloat16 [13312, 32, 4, 256], P('req', None, 'kv'), may hold values from -6 to 6
- page_table: int32 [1024, 20], P('req'), may hold values from 0 to 103, as said below
- lengths: int32 [1024], P('req'), may hold values from 256 to 639, as said below
- out_weight: bfloat16 [2048, 2048], P('kv'), may hold values from -0.5 to 0.5
- norm_gain: bfloat16 [2048], replicated, may hold values from 0.099609375 to 1.8984375
- router_weight: bfloat16 [64, 2048], replicated, may hold values from -0.03125 to 0.03125
- expert_ids: int32 [1024, 6], P('req'), may hold values from 0 to 63, all different within a row; in each aligned block of 8 rows (0 to 7, 8 to 15, ...) at most 2 rows name the same one
- expert_gate_up: bfloat16 [128, 2, 704, 2048], P('req', None, 'kv'), may hold values from -0.125 to 0.125
- expert_down: bfloat16 [128, 704, 2048], P('req', 'kv'), may hold values from -0.15625 to 0.15625
Outputs:
- out_hidden: bfloat16 [1024, 2048], P('req')
- updated_pool: bfloat16 [13312, 32, 4, 256], P('req', None, 'kv')
- hidden_norms: float32 [1024], P('req')
- max_logit: float32 [1024], P('req')
The draws below stay inside these ranges and needn't reach their ends.
Inputs may be any that keep to these rules, and one draw needn't show every extreme that they name: `page_table`: entries index the block of 104 pages of the request's own index of req. Requests of one index of req share their first pages, a common prompt of 8 or more pages; every other page is named by one request alone, and the page holding position lengths[r] is always one of request r's own. `lengths`: every request's length covers its shared prompt. `expert_ids`: within the 8 rows of one index of req, at most 2 rows name one expert, a bound that some block reaches of them.
All inputs are finite; a program needn't handle non-finite values.
Results may differ from the reference program's by a relative error of at most 0.015.
Values may be sent and summed in bfloat16 or wider, within the bound.
A program may use at most 64 MiB of HBM per device.

```python
import math
import jax
import jax.numpy as jnp
import numpy as np
from jax import lax

D = 2048
QUERY_HEADS = 16
KEY_VALUE_HEADS = 4
HEAD_SIZE = 128
FFE = 1408
TOPK = 6
SHARD_REQUESTS = 8
PAGE_TOKENS = 32
TABLE_PAGES = 20
SHARED_MIN = 8
EXPERTS = 64
CAP = 2
TOTAL_REQUESTS = 1024
PAGES_PER_SHARD = 104
TOTAL_PAGES = 13312
N_KV = 2


def layout(key):
    base = jax.random.fold_in(key, 71)
    first_key, second_key, third_key, fourth_key = jax.random.split(base, 4)
    shard_count = TOTAL_REQUESTS // SHARD_REQUESTS
    shared = jax.random.randint(first_key, (shard_count,), SHARED_MIN, TABLE_PAGES)
    perms = jax.vmap(lambda one_key: jax.random.permutation(one_key, PAGES_PER_SHARD))(jax.random.split(second_key, shard_count))
    request_ids = jnp.arange(TOTAL_REQUESTS, dtype=jnp.int32)
    device_ids = request_ids // SHARD_REQUESTS
    local_ids = request_ids % SHARD_REQUESTS
    shared_req = shared[device_ids]
    page_ids = jnp.arange(TABLE_PAGES, dtype=jnp.int32)
    own_index = shared_req[:, None] + local_ids[:, None] * (TABLE_PAGES - shared_req[:, None]) + page_ids[None, :] - shared_req[:, None]
    index = jnp.where(page_ids[None, :] < shared_req[:, None], page_ids[None, :], own_index)
    table = jnp.take_along_axis(perms[device_ids], index, axis=1)
    span = (TABLE_PAGES - shared_req) * PAGE_TOKENS
    extra = jax.random.randint(third_key, (TOTAL_REQUESTS,), 0, 1 << 20) % span
    lengths = shared_req * PAGE_TOKENS + extra
    longest = jax.random.randint(fourth_key, (), 0, TOTAL_REQUESTS)
    lengths = jnp.where(request_ids == longest, TABLE_PAGES * PAGE_TOKENS - 1, lengths)
    return (table.astype(jnp.int32), lengths.astype(jnp.int32))


def draw_page_table(key, part):
    return layout(key)[0]


def draw_lengths(key, part):
    return layout(key)[1]


def draw_kv_pool(key, part):
    own_key = jax.random.fold_in(key, 91)
    array_shape = (TOTAL_PAGES, PAGE_TOKENS, KEY_VALUE_HEADS, 2 * HEAD_SIZE)
    values = jnp.clip(jax.random.normal(own_key, array_shape, jnp.float32), -6.0, 6.0)
    return values.astype(jnp.bfloat16)


def draw_queries(key, part):
    own_key = jax.random.fold_in(key, 97)
    array_shape = (TOTAL_REQUESTS, QUERY_HEADS * HEAD_SIZE)
    values = jnp.clip(jax.random.normal(own_key, array_shape, jnp.float32), -6.0, 6.0)
    return values.astype(jnp.bfloat16)


def level_of(key, dims, pieces, smallest, top_value):
    loudness, own = 1.0, jax.random.fold_in(key, 6)
    for dim, parts in pieces:
        steps = jnp.exp(jax.random.uniform(jax.random.fold_in(own, dim), (parts,), jnp.float32, smallest / len(pieces), top_value / len(pieces)))
        loudness = loudness * jnp.repeat(steps, dims[dim] // parts).reshape([-1 if axis == dim else 1 for axis in range(len(dims))])
    return loudness


def assign_block(rng, own, number, rows, count, top, limit, slope):
    sequence = jax.random.permutation(rng, count)
    heavy_load, usual = portions_of(count, rows * top, limit, slope, True), portions_of(count, rows * top, limit, slope, False)
    places = jnp.arange(count)

    def named(sizes, rotation):
        used = int((sizes > 0).sum())
        fixed = max(1, used // 4)
        passed = fixed + (places - fixed + rotation * (used - fixed)) % max(1, count - fixed)
        return jnp.zeros((count,), jnp.int32).at[sequence[jnp.where(places < fixed, places, passed)]].set(jnp.asarray(sizes, jnp.int32))

    sizes = jnp.where(number % 4 == 0, named(heavy_load, number // 4), named(usual, number - number // 4 - 1))
    mixed = jax.random.permutation(jax.random.fold_in(own, 3), count)
    donor, sink = mixed[0:count // 2 * 2:2], mixed[1:count // 2 * 2:2]
    slack = jnp.minimum(sizes[donor] - 1, limit - sizes[sink]) // 2
    slack = jnp.where((donor == sequence[0]) | (sink == sequence[0]) | (sizes[sink] == 0), 0, jnp.maximum(slack, 0))
    passed = jax.random.randint(jax.random.fold_in(own, 4), (count // 2,), 0, 1 << 20) % (slack + 1)
    sizes = sizes.at[donor].add(-passed).at[sink].add(passed)
    members = jnp.searchsorted(jnp.cumsum(sizes), jnp.arange(rows * top), side="right").astype(jnp.int32)
    listing = members.reshape(top, rows).T
    listing = listing[jax.random.permutation(jax.random.fold_in(own, 1), rows)]
    rotation = jax.random.randint(jax.random.fold_in(own, 2), (rows, 1), 0, top)
    return jnp.take_along_axis(listing, (jnp.arange(top)[None, :] + rotation) % top, axis=1)


def portions_of(amount, total, limit, lean, full):
    portions = [(1 << 20) // math.isqrt(grade ** lean) + 1 for grade in range(1, amount + 1)]
    largest = limit if full else min(limit, max(-(-total // amount), total * portions[0] // sum(portions)))
    least = 1 if total - largest >= amount - 1 else 0
    given, spare = [largest] + [least] * (amount - 1), total - largest - least * (amount - 1)
    while spare > 0:
        free = [i for i in range(1, amount) if given[i] < largest] or [i for i in range(1, amount) if given[i] < limit]
        mass, left = sum([portions[i] for i in free]), spare
        for i in free:
            more = min(limit - given[i], max(1, left * portions[i] // mass), spare)
            given[i] = given[i] + more
            spare = spare - more
    return np.array(given)


def normal_values(key, dims, width, reach, pieces=(), kind=jnp.bfloat16):
    entries = width * jax.random.normal(key, dims, jnp.float32)
    if pieces:
        entries = entries * level_of(key, dims, pieces, -0.22, 0.18)
    return jnp.clip(entries, -reach, reach).astype(kind)


def setup_inputs(seed: int = 0) -> dict:
    keys = jax.random.split(jax.random.key(seed), 13)
    hidden = normal_values(keys[0], (TOTAL_REQUESTS, D), 0.3, 1.796875, ((0, 128),))
    queries = draw_queries(jax.random.fold_in(keys[12], 71), 0)
    fresh_key_value = normal_values(keys[2], (TOTAL_REQUESTS, KEY_VALUE_HEADS, 2 * HEAD_SIZE), 1.0, 6.0, ((0, 128), (1, 2)))
    kv_pool = draw_kv_pool(jax.random.fold_in(keys[12], 71), 0)
    page_table = draw_page_table(jax.random.fold_in(keys[12], 71), 0)
    lengths = draw_lengths(jax.random.fold_in(keys[12], 71), 0)
    out_weight = normal_values(keys[6], (QUERY_HEADS * HEAD_SIZE, D), HEAD_SIZE ** -0.5, 0.5, ((0, 2),))
    norm_gain = jnp.clip(1.0 + 0.18 * jax.random.normal(keys[7], (D,), jnp.float32), 0.099609375, 1.8984375).astype(jnp.bfloat16)
    router_weight = normal_values(keys[8], (EXPERTS, D), (16 * D) ** -0.5, 0.03125)
    expert_ids_keys = jax.random.split(jax.random.fold_in(keys[9], 1), TOTAL_REQUESTS // SHARD_REQUESTS)
    expert_ids_turns = jax.random.permutation(jax.random.fold_in(keys[9], 3), TOTAL_REQUESTS // SHARD_REQUESTS)
    expert_ids = jax.vmap(lambda own, number: assign_block(jax.random.fold_in(keys[9], 2), own, number, SHARD_REQUESTS, EXPERTS, TOPK, CAP, 2))(expert_ids_keys, expert_ids_turns).reshape((TOTAL_REQUESTS, TOPK))
    expert_gate_up = normal_values(keys[10], (2 * EXPERTS, 2, FFE // 2, D), D ** -0.5, 0.125, ((0, 128), (2, 2)))
    expert_down = normal_values(keys[11], (2 * EXPERTS, FFE // 2, D), FFE ** -0.5, 0.15625, ((0, 128), (1, 2)))
    return dict(hidden=hidden, queries=queries, fresh_key_value=fresh_key_value, kv_pool=kv_pool, page_table=page_table, lengths=lengths, out_weight=out_weight, norm_gain=norm_gain, router_weight=router_weight, expert_ids=expert_ids, expert_gate_up=expert_gate_up, expert_down=expert_down)


def reference(hidden, queries, fresh_key_value, kv_pool, page_table, lengths, out_weight, norm_gain, router_weight, expert_ids, expert_gate_up, expert_down):
    shard_count = TOTAL_REQUESTS // SHARD_REQUESTS
    request_ids = jnp.arange(TOTAL_REQUESTS, dtype=jnp.int32)
    slot_page = jnp.take_along_axis(page_table, (lengths // PAGE_TOKENS)[:, None].astype(jnp.int32), axis=1)[:, 0]
    global_page = request_ids // SHARD_REQUESTS * PAGES_PER_SHARD + slot_page
    refreshed_pool = kv_pool.at[global_page, lengths % PAGE_TOKENS].set(fresh_key_value)
    query_groups = QUERY_HEADS // KEY_VALUE_HEADS
    grouped_queries = queries.reshape(shard_count, SHARD_REQUESTS, KEY_VALUE_HEADS, query_groups, HEAD_SIZE)
    shard_page_pools = refreshed_pool.reshape(shard_count, PAGES_PER_SHARD, PAGE_TOKENS, KEY_VALUE_HEADS, 2 * HEAD_SIZE)
    tables = page_table.reshape(shard_count, SHARD_REQUESTS, TABLE_PAGES)
    device_lengths = lengths.reshape(shard_count, SHARD_REQUESTS)

    def attend_device(device_items):
        query_dev, shard_pool, shard_page_table, length_dev = device_items
        collected_pages = shard_pool[shard_page_table].reshape(SHARD_REQUESTS, TABLE_PAGES * PAGE_TOKENS, KEY_VALUE_HEADS, 2 * HEAD_SIZE)
        key_rows = collected_pages[..., :HEAD_SIZE].astype(jnp.float32)
        value_rows = collected_pages[..., HEAD_SIZE:].astype(jnp.float32)
        scores = jnp.einsum('rhgd,rphd->rhgp', query_dev.astype(jnp.float32), key_rows, precision=lax.Precision.HIGHEST) / math.sqrt(HEAD_SIZE)
        positions = jnp.arange(TABLE_PAGES * PAGE_TOKENS, dtype=jnp.int32)
        visible = positions[None, :] <= length_dev[:, None]
        scores = jnp.where(visible[:, None, None, :], scores, -1e+30)
        top_score = lax.optimization_barrier(jnp.max(scores, axis=-1))
        exponent = jnp.exp(scores - top_score[..., None])
        denominator = lax.optimization_barrier(jnp.sum(exponent, axis=-1))
        probs = lax.optimization_barrier(exponent.astype(jnp.bfloat16)).astype(jnp.float32)
        summed = jnp.einsum('rhgp,rphd->rhgd', probs, value_rows, precision=lax.Precision.HIGHEST)
        attended_dev = (summed / denominator[..., None]).astype(jnp.bfloat16)
        return attended_dev.reshape(SHARD_REQUESTS, QUERY_HEADS * HEAD_SIZE)
    attended = lax.map(attend_device, (grouped_queries, shard_page_pools, tables, device_lengths)).reshape(TOTAL_REQUESTS, QUERY_HEADS * HEAD_SIZE)
    projected = jnp.dot(attended, out_weight, preferred_element_type=jnp.float32)
    mixed_state = (hidden.astype(jnp.float32) + projected).astype(jnp.bfloat16)
    mixed_float = mixed_state.astype(jnp.float32)
    hidden_norms = jnp.sqrt(lax.optimization_barrier(jnp.mean(mixed_float * mixed_float, axis=-1)) + 1e-06)
    normed = (mixed_float / hidden_norms[:, None] * norm_gain.astype(jnp.float32)).astype(jnp.bfloat16)
    logits = jnp.dot(normed, router_weight.T, preferred_element_type=jnp.float32)
    max_logit = lax.optimization_barrier(jnp.max(logits, axis=-1))
    onehot = expert_ids[:, :, None] == jnp.arange(EXPERTS, dtype=jnp.int32)[None, None, :]
    picked = lax.optimization_barrier(jnp.sum(jnp.where(onehot, logits[:, None, :], 0.0), axis=-1))
    exponent = jnp.exp(picked)
    gate_weights = exponent / lax.optimization_barrier(jnp.sum(exponent, axis=-1, keepdims=True))
    flat_hot = onehot.reshape(shard_count, SHARD_REQUESTS * TOPK, EXPERTS)
    counts = jnp.cumsum(flat_hot.astype(jnp.int32), axis=1)
    slot_rank = (lax.optimization_barrier(jnp.sum(jnp.where(flat_hot, counts, 0), axis=-1)) - 1).reshape(TOTAL_REQUESTS, TOPK)
    source = request_ids // SHARD_REQUESTS
    buffer_row = source[:, None] * CAP + slot_rank
    buffers = jnp.zeros((EXPERTS, shard_count * CAP, D), jnp.bfloat16)
    buffers = buffers.at[expert_ids, buffer_row].set(jnp.broadcast_to(normed[:, None, :], (TOTAL_REQUESTS, TOPK, D)))
    block_units = FFE // (2 * N_KV)
    gate_blocks = expert_gate_up.reshape(EXPERTS, 2, 2, N_KV, block_units, D)
    gate_blocks = jnp.transpose(gate_blocks, (0, 1, 3, 2, 4, 5)).reshape(EXPERTS, 2 * N_KV, 2, block_units, D)
    down_blocks = expert_down.reshape(EXPERTS, 2 * N_KV, block_units, D)

    def expert(expert_items):
        rows, gate_up, down = expert_items

        def one_block(block_gate, block_down):
            gate_proj = jnp.dot(rows, block_gate[0].T, preferred_element_type=jnp.float32)
            up_proj = jnp.dot(rows, block_gate[1].T, preferred_element_type=jnp.float32)
            activated = (jax.nn.silu(gate_proj) * up_proj).astype(jnp.bfloat16)
            return jnp.dot(activated, block_down, preferred_element_type=jnp.float32).astype(jnp.bfloat16)
        block_outs = jax.vmap(one_block)(gate_up, down)
        return lax.optimization_barrier(jnp.sum(block_outs.astype(jnp.float32), axis=0))
    results = lax.map(expert, (buffers, gate_blocks, down_blocks))
    expert_out = results[expert_ids, buffer_row]
    routed = lax.optimization_barrier(jnp.sum(gate_weights[..., None] * expert_out, axis=1))
    out_hidden = (mixed_float + routed).astype(jnp.bfloat16)
    return (out_hidden, refreshed_pool, hidden_norms, max_logit)
```

```python
import functools
import math

import jax
import jax.numpy as jnp
from jax import lax
from jax.experimental import pallas as pl
from jax.experimental.pallas import tpu as pltpu
from jax.sharding import PartitionSpec as P

MESH = pl.DeviceIdType.MESH
F32 = jnp.float32
BF16 = jnp.bfloat16


def dot_nn(a, b):
    return lax.dot_general(a, b, (((1,), (0,)), ((), ())), preferred_element_type=F32)


def dot_nt(a, b):
    return lax.dot_general(a, b, (((1,), (1,)), ((), ())), preferred_element_type=F32)


def attention_kernel(
    page_len,
    table_s,
    lens_s,
    table_v,
    lens_v,
    q_ref,
    fresh_ref,
    pool_hbm,
    ow_hbm,
    pool_out,
    part_ref,
    kv,
    ow,
    scores,
    weight,
    in_sem,
    ow_sem,
    out_sem,
):
    reqs, max_pages = table_v.shape
    rows = kv.shape[0]
    page_rows = 4 * page_len
    pages = rows // page_rows
    chunks = in_sem.shape[0]
    chunk = rows // chunks
    ow_chunks = ow_sem.shape[0]
    ow_chunk = ow.shape[0] // ow_chunks
    loads = [
        pltpu.make_async_copy(
            pool_hbm.at[pl.ds(i * chunk, chunk)], kv.at[pl.ds(i * chunk, chunk)], in_sem.at[i]
        )
        for i in range(chunks)
    ]
    ow_loads = [
        pltpu.make_async_copy(
            ow_hbm.at[pl.ds(i * ow_chunk, ow_chunk)],
            ow.at[pl.ds(i * ow_chunk, ow_chunk)],
            ow_sem.at[i],
        )
        for i in range(ow_chunks)
    ]
    for copy in loads + ow_loads:
        copy.start()

    lens = lens_v[...]
    last_page = lens // page_len
    rem = lens % page_len
    lane = lax.broadcasted_iota(jnp.int32, (reqs, page_rows), 1)
    whole = jnp.zeros((reqs, page_rows), F32)
    partial = jnp.zeros((reqs, page_rows), F32)
    for j in range(max_pages):
        named = lane == table_v[:, j : j + 1]
        whole += jnp.where(named & (last_page > j), 1.0, 0.0)
        partial += jnp.where(named & (last_page == j), 1.0, 0.0)
    seen = (lane // 4) <= rem
    is_key = (lane % 4) < 2
    for head in range(2):
        mine = is_key & ((lane % 2) == head)
        full_mask = jnp.where(mine, 1.0, 0.0)
        part_mask = jnp.where(mine & seen, 1.0, 0.0)
        for p in range(pages):
            weight[p, head] = (
                whole[:, p : p + 1] * full_mask + partial[:, p : p + 1] * part_mask
            )

    query = q_ref[...].astype(F32)
    head_dim = kv.shape[1]
    heads = query.shape[1] // head_dim
    group = heads // 2
    stacked = jnp.concatenate(
        [query[:, h * head_dim : (h + 1) * head_dim] for h in range(heads)], axis=0
    ).astype(BF16)
    scale = 1.0 / math.sqrt(head_dim)

    for copy in loads:
        copy.wait()
    row = lax.broadcasted_iota(jnp.int32, (16, head_dim), 0)
    for r in range(reqs):
        length = lens_s[r]
        page = table_s[r, length // page_len]
        position = page * page_len + length % page_len
        base = pl.multiple_of((position // 4) * 16, 16)
        four = fresh_ref[4 * r : 4 * r + 4, :].astype(F32)
        tiled = jnp.concatenate([four, four, four, four], axis=0)
        old = kv[pl.ds(base, 16), :].astype(F32)
        kv[pl.ds(base, 16), :] = jnp.where(row // 4 == position % 4, tiled, old).astype(BF16)
    stores = [
        pltpu.make_async_copy(
            kv.at[pl.ds(i * chunk, chunk)], pool_out.at[pl.ds(i * chunk, chunk)], out_sem.at[i]
        )
        for i in range(chunks)
    ]
    for copy in stores:
        copy.start()

    span = 8
    groups = pages // span

    def score_group(g, top):
        block = kv[pl.ds(pl.multiple_of(g * span * page_rows, span * page_rows), span * page_rows), :]
        s = dot_nt(stacked, block)
        tops = [top[h * reqs : (h + 1) * reqs, :] for h in range(heads)]
        for i in range(span):
            p = g * span + i
            for h in range(heads):
                w = weight[p, h // group]
                piece = s[h * reqs : (h + 1) * reqs, i * page_rows : (i + 1) * page_rows]
                masked = jnp.where(w > 0, piece * scale, -1e30)
                scores[p, h * reqs : (h + 1) * reqs, :] = masked
                tops[h] = jnp.maximum(tops[h], masked)
        return jnp.concatenate(tops, axis=0)

    top = lax.fori_loop(
        0, groups, score_group, jnp.full((heads * reqs, page_rows), -1e30, F32)
    )
    top = jnp.max(top, axis=1, keepdims=True)

    def value_group(g, carry):
        total, acc = carry
        parts = []
        for i in range(span):
            p = g * span + i
            w = jnp.concatenate(
                [weight[p, h // group] for h in range(heads)], axis=0
            )
            e = jnp.exp(scores[p] - top) * w
            total += e
            parts.append(pltpu.roll(e, 2, 1).astype(BF16))
        block = kv[pl.ds(pl.multiple_of(g * span * page_rows, span * page_rows), span * page_rows), :]
        acc += dot_nn(jnp.concatenate(parts, axis=1), block)
        return total, acc

    total, acc = lax.fori_loop(
        0,
        groups,
        value_group,
        (
            jnp.zeros((heads * reqs, page_rows), F32),
            jnp.zeros((heads * reqs, head_dim), F32),
        ),
    )
    result = acc / jnp.sum(total, axis=1, keepdims=True)
    attended = jnp.concatenate(
        [result[h * reqs : (h + 1) * reqs, :] for h in range(heads)], axis=1
    ).astype(BF16)
    for copy in ow_loads:
        copy.wait()
    part_ref[...] = dot_nn(attended, ow[...]).astype(BF16)
    for copy in stores:
        copy.wait()


def expert_kernel(
    part_ref,
    hidden_ref,
    gain_ref,
    router_ref,
    ids_ref,
    gu_hbm,
    down_hbm,
    out_ref,
    norm_ref,
    logit_ref,
    gu,
    down,
    pbuf,
    router2,
    zbuf,
    psend,
    xbuf,
    ysend,
    ybuf,
    rsend,
    rbuf,
    csend,
    fbuf,
    osend,
    obuf,
    w_sem,
    kv_sem,
    z_send,
    z_recv,
    p_send,
    p_recv,
    s_send,
    s_recv,
    y_sem,
    r_send,
    r_recv,
    c_send,
    c_recv,
    o_sem,
):
    me = lax.axis_index("req")
    k = lax.axis_index("kv")
    core = me % 2
    xh = (me // 2) % 2
    y = (me // 4) % 4
    z = me // 16
    line = y * 2 + xh
    sibling = me + 1 - 2 * core

    def plane_peer(i):
        py = (y + i // 4) % 4
        px = (xh + (i // 2) % 2) % 2
        pk = (k + i % 2) % 2
        return z * 16 + py * 4 + px * 2 + core, pk, py * 2 + px

    def z_peer(d):
        return ((z + d) % 8) * 16 + me % 16

    barrier = pltpu.get_barrier_semaphore()
    for i in range(1, 16):
        dev, pk, _ = plane_peer(i)
        pl.semaphore_signal(barrier, inc=1, device_id=(dev, pk), device_id_type=MESH)
    for d in range(1, 8):
        pl.semaphore_signal(barrier, inc=1, device_id=(z_peer(d), k), device_id_type=MESH)
    pl.semaphore_signal(barrier, inc=1, device_id=(sibling, k), device_id_type=MESH)

    w_loads = [
        pltpu.make_async_copy(gu_hbm.at[0], gu.at[0], w_sem.at[0]),
        pltpu.make_async_copy(gu_hbm.at[1], gu.at[1], w_sem.at[1]),
        pltpu.make_async_copy(down_hbm, down, w_sem.at[2]),
    ]
    for copy in w_loads:
        copy.start()
    pl.semaphore_wait(barrier, 23)

    swap = pltpu.make_async_remote_copy(
        src_ref=part_ref,
        dst_ref=pbuf,
        send_sem=kv_sem.at[0],
        recv_sem=kv_sem.at[1],
        device_id=(me, 1 - k),
        device_id_type=MESH,
    )
    swap.start()
    tokens, width = hidden_ref.shape
    half = width // 2
    experts = router_ref.shape[0]
    chosen_count = ids_ref.shape[1]
    router2[0:experts, :] = router_ref[...]
    router2[experts : 2 * experts, :] = router_ref[...]
    lane = lax.broadcasted_iota(jnp.int32, (tokens, 2 * experts), 1)
    chosen = jnp.zeros((tokens, 2 * experts), F32)
    for j in range(chosen_count):
        chosen += jnp.where(lane % experts == ids_ref[:, j : j + 1], 1.0, 0.0)
    swap.wait()
    projected = part_ref[...].astype(F32) + pbuf[...].astype(F32)
    mixed = (hidden_ref[...].astype(F32) + projected).astype(BF16).astype(F32)
    norms = jnp.sqrt(jnp.sum(mixed * mixed, axis=1, keepdims=True) / width + 1e-06)
    normed = (mixed / norms * gain_ref[...].astype(F32)).astype(BF16)
    logits = dot_nt(normed, router2[...])
    norm_ref[...] = jnp.broadcast_to(norms, norm_ref.shape)
    logit_ref[...] = jnp.broadcast_to(jnp.max(logits, axis=1, keepdims=True), logit_ref.shape)
    raised = jnp.where(chosen > 0, jnp.exp(logits), 0.0)
    gates = raised / jnp.sum(jnp.where(lane < experts, raised, 0.0), axis=1, keepdims=True)
    high = gates.astype(BF16).astype(F32)
    meta = jnp.where(lane < experts, jnp.where(chosen > 0, high, -1.0), gates - high)

    normed32 = normed.astype(F32)
    own_half = jnp.where(k == 0, normed32[:, :half], normed32[:, half:])
    zbuf[z] = jnp.concatenate([own_half, meta], axis=1).astype(BF16)
    z_copies = []
    for d in range(1, 8):
        copy = pltpu.make_async_remote_copy(
            src_ref=zbuf.at[z],
            dst_ref=zbuf.at[z],
            send_sem=z_send.at[d],
            recv_sem=z_recv.at[d],
            device_id=(z_peer(d), k),
            device_id_type=MESH,
        )
        copy.start()
        z_copies.append(copy)

    count = 8 * tokens
    slots = 128
    row = lax.broadcasted_iota(jnp.int32, (slots, 2 * experts), 0)
    col = lax.broadcasted_iota(jnp.int32, (slots, 2 * experts), 1)
    pick_high = jnp.where(col == 8 * z + row // 16, 1.0, 0.0).astype(BF16)
    pick_low = jnp.where(col == experts + 8 * z + row // 16, 1.0, 0.0).astype(BF16)
    row = lax.broadcasted_iota(jnp.int32, (count, count), 0)
    col = lax.broadcasted_iota(jnp.int32, (count, count), 1)
    same = row // tokens == col // tokens
    before = jnp.where(same & (row < col), 1.0, 0.0).astype(BF16)
    after = jnp.where(same & (col < row), 1.0, 0.0).astype(BF16)

    for copy in z_copies:
        copy.wait()
    gathered = zbuf[...].astype(F32).reshape(count, half + 2 * experts)
    metas = gathered[:, half:].astype(BF16)
    states = gathered[:, :half].astype(BF16)
    row = lax.broadcasted_iota(jnp.int32, (slots, count), 0)
    col = lax.broadcasted_iota(jnp.int32, (slots, count), 1)
    taken = jnp.where(dot_nt(pick_high, metas) >= 0, 1.0, 0.0)
    rank = dot_nn(taken.astype(BF16), before)
    hit = (taken > 0) & (col // tokens == (row // 2) % 8) & (rank == (row % 2).astype(F32))
    spread = dot_nn(jnp.where(hit, 1.0, 0.0).astype(BF16), states)
    psend[...] = spread.reshape(8, 16, half).astype(BF16)
    p_copies = []
    for i in range(1, 16):
        dev, pk, block = plane_peer(i)
        copy = pltpu.make_async_remote_copy(
            src_ref=psend.at[block],
            dst_ref=xbuf.at[core, k, line],
            send_sem=p_send.at[i],
            recv_sem=p_recv.at[i],
            device_id=(dev, pk),
            device_id_type=MESH,
        )
        copy.start()
        p_copies.append(copy)
    xbuf[core, k, line] = psend[line]

    row = lax.broadcasted_iota(jnp.int32, (count, slots), 0)
    col = lax.broadcasted_iota(jnp.int32, (count, slots), 1)
    gate_high = dot_nt(metas, pick_high)
    gate_low = dot_nt(metas, pick_low)
    taken = jnp.where(gate_high >= 0, 1.0, 0.0)
    rank = dot_nn(after, taken.astype(BF16))
    hit = (taken > 0) & (row // tokens == (col // 2) % 8) & (rank == (col % 2).astype(F32))
    combine_high = jnp.where(hit, gate_high, 0.0).astype(BF16)
    combine_low = jnp.where(hit, gate_low, 0.0).astype(BF16)

    s_copies = []
    for i in range(16):
        if i > 0:
            p_copies[i - 1].wait()
        sy = (y + 4 - i // 4) % 4
        sx = (xh + (i // 2) % 2) % 2
        sk = (k + i % 2) % 2
        copy = pltpu.make_async_remote_copy(
            src_ref=xbuf.at[core, sk, sy * 2 + sx],
            dst_ref=xbuf.at[core, sk, sy * 2 + sx],
            send_sem=s_send.at[i],
            recv_sem=s_recv.at[i],
            device_id=(sibling, k),
            device_id_type=MESH,
        )
        copy.start()
        s_copies.append(copy)
    for copy in w_loads:
        copy.wait()
    for copy in s_copies:
        copy.wait()

    def feed_forward(side):
        left = xbuf[side, 0].astype(F32).reshape(slots, half).astype(BF16)
        right = xbuf[side, 1].astype(F32).reshape(slots, half).astype(BF16)
        gate = dot_nt(left, gu[0, :, :half]) + dot_nt(right, gu[0, :, half:])
        up = dot_nt(left, gu[1, :, :half]) + dot_nt(right, gu[1, :, half:])
        activated = (gate / (1.0 + jnp.exp(-gate)) * up).astype(BF16)
        return dot_nn(activated, down[...])

    ysend[...] = feed_forward(1 - core).astype(BF16)
    trade = pltpu.make_async_remote_copy(
        src_ref=ysend,
        dst_ref=ybuf,
        send_sem=y_sem.at[0],
        recv_sem=y_sem.at[1],
        device_id=(sibling, k),
        device_id_type=MESH,
    )
    trade.start()
    own = feed_forward(core)
    trade.wait()
    both = own + ybuf[...].astype(F32)
    rsend[0] = both[:, :half].reshape(8, 16, half).astype(BF16)
    rsend[1] = both[:, half:].reshape(8, 16, half).astype(BF16)
    r_copies = []
    for i in range(1, 16):
        dev, pk, block = plane_peer(i)
        copy = pltpu.make_async_remote_copy(
            src_ref=rsend.at[pk, block],
            dst_ref=rbuf.at[k, line],
            send_sem=r_send.at[i],
            recv_sem=r_recv.at[i],
            device_id=(dev, pk),
            device_id_type=MESH,
        )
        copy.start()
        r_copies.append(copy)
    rbuf[k, line] = rsend[k, line]
    for copy in r_copies:
        copy.wait()
    routed = jnp.zeros((count, half), F32)
    for side in range(2):
        arrived = rbuf[side].astype(F32).reshape(slots, half).astype(BF16)
        routed += dot_nn(combine_high, arrived) + dot_nn(combine_low, arrived)
    csend[...] = routed.reshape(8, tokens, half).astype(BF16)
    c_copies = []
    for d in range(1, 8):
        copy = pltpu.make_async_remote_copy(
            src_ref=csend.at[(z + d) % 8],
            dst_ref=fbuf.at[z],
            send_sem=c_send.at[d],
            recv_sem=c_recv.at[d],
            device_id=(z_peer(d), k),
            device_id_type=MESH,
        )
        copy.start()
        c_copies.append(copy)
    fbuf[z] = csend[z]
    for copy in c_copies:
        copy.wait()
    total = jnp.sum(fbuf[...].astype(F32), axis=0)
    own_mixed = jnp.where(k == 0, mixed[:, :half], mixed[:, half:])
    mine = (own_mixed + total).astype(BF16)
    osend[...] = mine
    final = pltpu.make_async_remote_copy(
        src_ref=osend,
        dst_ref=obuf,
        send_sem=o_sem.at[0],
        recv_sem=o_sem.at[1],
        device_id=(me, 1 - k),
        device_id_type=MESH,
    )
    final.start()
    final.wait()
    mine32, other32 = mine.astype(F32), obuf[...].astype(F32)
    out_ref[:, :half] = jnp.where(k == 0, mine32, other32).astype(BF16)
    out_ref[:, half:] = jnp.where(k == 0, other32, mine32).astype(BF16)


def to_rows(array):
    lead = math.prod(array.shape[:-2])
    head_dim = array.shape[-1] // 2
    split = array.reshape(lead, array.shape[-2], 2, head_dim)
    return split.transpose(0, 2, 1, 3).reshape(-1, head_dim)


def body(
    hidden,
    queries,
    fresh_key_value,
    kv_pool,
    page_table,
    lengths,
    out_weight,
    norm_gain,
    router_weight,
    expert_ids,
    expert_gate_up,
    expert_down,
):
    tokens, width = hidden.shape
    half = width // 2
    pages, page_len, kv_heads, pair = kv_pool.shape
    head_dim = pair // 2
    pool_rows = to_rows(kv_pool)
    fresh_rows = to_rows(fresh_key_value)
    rows = pool_rows.shape[0]
    heads = queries.shape[1] // head_dim
    page_rows = rows // pages
    vmem = pl.BlockSpec(memory_space=pltpu.VMEM)
    smem = pl.BlockSpec(memory_space=pltpu.SMEM)
    hbm = pl.BlockSpec(memory_space=pltpu.HBM)
    pool_new, part = pl.pallas_call(
        functools.partial(attention_kernel, page_len),
        out_shape=(
            jax.ShapeDtypeStruct(pool_rows.shape, BF16),
            jax.ShapeDtypeStruct((tokens, width), BF16),
        ),
        in_specs=[smem, smem, vmem, vmem, vmem, vmem, hbm, hbm],
        out_specs=(hbm, vmem),
        scratch_shapes=[
            pltpu.VMEM(pool_rows.shape, BF16),
            pltpu.VMEM(out_weight.shape, BF16),
            pltpu.VMEM((pages, heads * tokens, page_rows), F32),
            pltpu.VMEM((pages, 2, tokens, page_rows), F32),
            pltpu.SemaphoreType.DMA((8,)),
            pltpu.SemaphoreType.DMA((4,)),
            pltpu.SemaphoreType.DMA((8,)),
        ],
    )(
        page_table,
        lengths,
        page_table,
        lengths.reshape(tokens, 1),
        queries,
        fresh_rows,
        pool_rows,
        out_weight,
    )
    updated_pool = (
        pool_new.reshape(pages * page_len, 2, kv_heads, head_dim)
        .transpose(0, 2, 1, 3)
        .reshape(kv_pool.shape)
    )
    gate_up = expert_gate_up[0]
    down = expert_down[0]
    experts = router_weight.shape[0]
    dma = pltpu.SemaphoreType.DMA
    out_hidden, norms, max_logit = pl.pallas_call(
        expert_kernel,
        out_shape=(
            jax.ShapeDtypeStruct((tokens, width), BF16),
            jax.ShapeDtypeStruct((tokens, 128), F32),
            jax.ShapeDtypeStruct((tokens, 128), F32),
        ),
        in_specs=[vmem, vmem, vmem, vmem, vmem, hbm, hbm],
        out_specs=(vmem, vmem, vmem),
        scratch_shapes=[
            pltpu.VMEM(gate_up.shape, BF16),
            pltpu.VMEM(down.shape, BF16),
            pltpu.VMEM((tokens, width), BF16),
            pltpu.VMEM((2 * experts, width), BF16),
            pltpu.VMEM((8, tokens, half + 2 * experts), BF16),
            pltpu.VMEM((8, 16, half), BF16),
            pltpu.VMEM((2, 2, 8, 16, half), BF16),
            pltpu.VMEM((128, width), BF16),
            pltpu.VMEM((128, width), BF16),
            pltpu.VMEM((2, 8, 16, half), BF16),
            pltpu.VMEM((2, 8, 16, half), BF16),
            pltpu.VMEM((8, tokens, half), BF16),
            pltpu.VMEM((8, tokens, half), BF16),
            pltpu.VMEM((tokens, half), BF16),
            pltpu.VMEM((tokens, half), BF16),
            dma((3,)),
            dma((2,)),
            dma((8,)),
            dma((8,)),
            dma((16,)),
            dma((16,)),
            dma((16,)),
            dma((16,)),
            dma((2,)),
            dma((16,)),
            dma((16,)),
            dma((8,)),
            dma((8,)),
            dma((2,)),
        ],
        compiler_params=pltpu.CompilerParams(collective_id=0, has_side_effects=True),
    )(part, hidden, norm_gain.reshape(1, width), router_weight, expert_ids, gate_up, down)
    return (out_hidden, updated_pool, norms[:, 0], max_logit[:, 0])


def solution(mesh):
    in_specs = (
        P("req", None),
        P("req", "kv"),
        P("req", "kv", None),
        P("req", None, "kv", None),
        P("req", None),
        P("req"),
        P("kv", None),
        P(),
        P(),
        P("req", None),
        P("req", None, "kv", None),
        P("req", "kv", None),
    )
    out_specs = (P("req", None), P("req", None, "kv", None), P("req"), P("req"))
    return jax.shard_map(body, mesh=mesh, in_specs=in_specs, out_specs=out_specs, check_vma=False)
```

```python
import functools
import math

import jax
import jax.numpy as jnp
from jax import lax
from jax.experimental import pallas as pl
from jax.experimental.pallas import tpu as pltpu
from jax.sharding import PartitionSpec as P

MESH = pl.DeviceIdType.MESH
F32 = jnp.float32
BF16 = jnp.bfloat16


def dot_nn(a, b):
    return lax.dot_general(a, b, (((1,), (0,)), ((), ())), preferred_element_type=F32)


def dot_nt(a, b):
    return lax.dot_general(a, b, (((1,), (1,)), ((), ())), preferred_element_type=F32)


def pool_kernel(page_len, table_s, lens_s, fresh_ref, pool_hbm, pool_out, kv, in_sem, out_sem):
    reqs = table_s.shape[0]
    head_dim = kv.shape[1]
    chunks = in_sem.shape[0]
    chunk = kv.shape[0] // chunks
    loads = [
        pltpu.make_async_copy(
            pool_hbm.at[pl.ds(i * chunk, chunk)], kv.at[pl.ds(i * chunk, chunk)], in_sem.at[i]
        )
        for i in range(chunks)
    ]
    for copy in loads:
        copy.start()
    row = lax.broadcasted_iota(jnp.int32, (16, head_dim), 0)
    bases, news = [], []
    for r in range(reqs):
        length = lens_s[r]
        page = table_s[r, length // page_len]
        position = page * page_len + length % page_len
        bases.append(position // 4)
        four = fresh_ref[4 * r : 4 * r + 4, :].astype(F32)
        news.append((row // 4 == position % 4, jnp.concatenate([four, four, four, four], axis=0)))
    stores = []
    for i in range(chunks):
        loads[i].wait()
        for r in range(reqs):

            @pl.when(bases[r] // (chunk // 16) == i)
            def _():
                base = pl.multiple_of(bases[r] * 16, 16)
                hit, tiled = news[r]
                old = kv[pl.ds(base, 16), :].astype(F32)
                kv[pl.ds(base, 16), :] = jnp.where(hit, tiled, old).astype(BF16)

        copy = pltpu.make_async_copy(
            kv.at[pl.ds(i * chunk, chunk)], pool_out.at[pl.ds(i * chunk, chunk)], out_sem.at[i]
        )
        copy.start()
        stores.append(copy)
    for copy in stores:
        copy.wait()


def attend(page_len, table_v, lens_s, q_ref, kv, scores, weight, loads):
    reqs, max_pages = table_v.shape
    head_dim = kv.shape[1]
    page_rows = 4 * page_len
    pages = kv.shape[0] // page_rows
    req_row = lax.broadcasted_iota(jnp.int32, (reqs, page_rows), 0)
    lane = lax.broadcasted_iota(jnp.int32, (reqs, page_rows), 1)
    lens = jnp.zeros((reqs, page_rows), jnp.int32)
    for r in range(reqs):
        lens = jnp.where(req_row == r, lens_s[r], lens)
    last_page = lens // page_len
    rem = lens % page_len
    whole = jnp.zeros((reqs, page_rows), F32)
    partial = jnp.zeros((reqs, page_rows), F32)
    for j in range(max_pages):
        named = lane == table_v[:, j : j + 1]
        whole += jnp.where(named & (last_page > j), 1.0, 0.0)
        partial += jnp.where(named & (last_page == j), 1.0, 0.0)
    seen = (lane // 4) <= rem
    is_key = (lane % 4) < 2
    masks = []
    for head in range(2):
        mine = is_key & ((lane % 2) == head)
        masks.append((jnp.where(mine, 1.0, 0.0), jnp.where(mine & seen, 1.0, 0.0)))
    for p in range(pages):
        full = jnp.broadcast_to(whole[:, p : p + 1], (reqs, page_rows))
        part = jnp.broadcast_to(partial[:, p : p + 1], (reqs, page_rows))
        for head in range(2):
            weight[p, head] = full * masks[head][0] + part * masks[head][1]

    query = q_ref[...].astype(F32)
    heads = query.shape[1] // head_dim
    group = heads // 2
    stacked = jnp.concatenate(
        [query[:, h * head_dim : (h + 1) * head_dim] for h in range(heads)], axis=0
    ).astype(BF16)
    scale = 1.0 / math.sqrt(head_dim)
    for copy in loads:
        copy.wait()
    span = 8
    groups = pages // span
    rows = span * page_rows

    def score_group(g, top):
        block = kv[pl.ds(pl.multiple_of(g * rows, rows), rows), :]
        s = dot_nt(stacked, block)
        tops = [top[h * reqs : (h + 1) * reqs, :] for h in range(heads)]
        for i in range(span):
            p = g * span + i
            for h in range(heads):
                w = weight[p, h // group]
                piece = s[h * reqs : (h + 1) * reqs, i * page_rows : (i + 1) * page_rows]
                masked = jnp.where(w > 0, piece, -1e30)
                scores[p, h * reqs : (h + 1) * reqs, :] = masked
                tops[h] = jnp.maximum(tops[h], masked)
        return jnp.concatenate(tops, axis=0)

    def value_group(g, carry):
        total, acc = carry
        parts = []
        for i in range(span):
            p = g * span + i
            w = jnp.concatenate([weight[p, h // group] for h in range(heads)], axis=0)
            e = jnp.exp((scores[p] - top) * scale) * w
            total += e
            parts.append(pltpu.roll(e, 2, 1).astype(BF16))
        block = kv[pl.ds(pl.multiple_of(g * rows, rows), rows), :]
        acc += dot_nn(jnp.concatenate(parts, axis=1), block)
        return total, acc

    top = jnp.full((heads * reqs, page_rows), -1e30, F32)
    for g in range(groups):
        top = score_group(g, top)
    top = jnp.max(top, axis=1, keepdims=True)
    carry = (
        jnp.zeros((heads * reqs, page_rows), F32),
        jnp.zeros((heads * reqs, head_dim), F32),
    )
    for g in range(groups):
        carry = value_group(g, carry)
    total, acc = carry
    result = acc / jnp.sum(total, axis=1, keepdims=True)
    return jnp.concatenate(
        [result[h * reqs : (h + 1) * reqs, :] for h in range(heads)], axis=1
    ).astype(BF16)


def expert_kernel(
    page_len,
    lens_s,
    table_v,
    q_ref,
    hidden_ref,
    gain_ref,
    router_ref,
    ids_ref,
    pool_hbm,
    ow_hbm,
    gu_hbm,
    down_hbm,
    out_ref,
    stat_ref,
    kv,
    ow,
    scores,
    weight,
    part_ref,
    gu,
    down,
    pbuf,
    router2,
    zbuf,
    psend,
    xbuf,
    ysend,
    ybuf,
    rsend,
    rbuf,
    csend,
    fbuf,
    osend,
    obuf,
    w_sem,
    kv_sem,
    z_send,
    z_recv,
    p_send,
    p_recv,
    s_send,
    s_recv,
    y_sem,
    r_send,
    r_recv,
    c_send,
    c_recv,
    o_sem,
    in_sem,
    ow_sem,
):
    me = lax.axis_index("req")
    k = lax.axis_index("kv")
    core = me % 2
    xh = (me // 2) % 2
    y = (me // 4) % 4
    z = me // 16
    line = y * 2 + xh
    sibling = me + 1 - 2 * core

    def plane_peer(i):
        py = (y + i // 4) % 4
        px = (xh + (i // 2) % 2) % 2
        pk = (k + i % 2) % 2
        return z * 16 + py * 4 + px * 2 + core, pk, py * 2 + px

    def z_peer(d):
        return ((z + d) % 8) * 16 + me % 16

    barrier = pltpu.get_barrier_semaphore()
    for i in range(1, 16):
        dev, pk, _ = plane_peer(i)
        pl.semaphore_signal(barrier, inc=1, device_id=(dev, pk), device_id_type=MESH)
    for d in range(1, 8):
        pl.semaphore_signal(barrier, inc=1, device_id=(z_peer(d), k), device_id_type=MESH)
    pl.semaphore_signal(barrier, inc=1, device_id=(sibling, k), device_id_type=MESH)

    chunks = in_sem.shape[0]
    chunk = kv.shape[0] // chunks
    loads = [
        pltpu.make_async_copy(
            pool_hbm.at[pl.ds(i * chunk, chunk)], kv.at[pl.ds(i * chunk, chunk)], in_sem.at[i]
        )
        for i in range(chunks)
    ]
    ow_chunks = ow_sem.shape[0]
    ow_chunk = ow.shape[0] // ow_chunks
    ow_loads = [
        pltpu.make_async_copy(
            ow_hbm.at[pl.ds(i * ow_chunk, ow_chunk)],
            ow.at[pl.ds(i * ow_chunk, ow_chunk)],
            ow_sem.at[i],
        )
        for i in range(ow_chunks)
    ]
    w_loads = [
        pltpu.make_async_copy(gu_hbm.at[0], gu.at[0], w_sem.at[0]),
        pltpu.make_async_copy(gu_hbm.at[1], gu.at[1], w_sem.at[1]),
        pltpu.make_async_copy(down_hbm, down, w_sem.at[2]),
    ]
    for copy in loads + ow_loads + w_loads:
        copy.start()
    attended = attend(page_len, table_v, lens_s, q_ref, kv, scores, weight, loads)
    for copy in ow_loads:
        copy.wait()
    part_ref[...] = dot_nn(attended, ow[...]).astype(BF16)
    pl.semaphore_wait(barrier, 23)

    swap = pltpu.make_async_remote_copy(
        src_ref=part_ref,
        dst_ref=pbuf,
        send_sem=kv_sem.at[0],
        recv_sem=kv_sem.at[1],
        device_id=(me, 1 - k),
        device_id_type=MESH,
    )
    swap.start()
    tokens, width = hidden_ref.shape
    half = width // 2
    experts = router_ref.shape[0]
    chosen_count = ids_ref.shape[1]
    router2[0:experts, :] = router_ref[...]
    router2[experts : 2 * experts, :] = router_ref[...]
    lane = lax.broadcasted_iota(jnp.int32, (tokens, 2 * experts), 1)
    chosen = jnp.zeros((tokens, 2 * experts), F32)
    for j in range(chosen_count):
        chosen += jnp.where(lane % experts == ids_ref[:, j : j + 1], 1.0, 0.0)
    swap.wait()
    projected = part_ref[...].astype(F32) + pbuf[...].astype(F32)
    mixed = (hidden_ref[...].astype(F32) + projected).astype(BF16).astype(F32)
    norms = jnp.sqrt(jnp.sum(mixed * mixed, axis=1, keepdims=True) / width + 1e-06)
    normed = (mixed / norms * gain_ref[...].astype(F32).reshape(1, width)).astype(BF16)
    logits = dot_nt(normed, router2[...])
    stat_ref[...] = jnp.where(
        lane == 0, norms, jnp.max(logits, axis=1, keepdims=True)
    )
    raised = jnp.where(chosen > 0, jnp.exp(logits), 0.0)
    gates = raised / jnp.sum(jnp.where(lane < experts, raised, 0.0), axis=1, keepdims=True)
    high = gates.astype(BF16).astype(F32)
    meta = jnp.where(lane < experts, jnp.where(chosen > 0, high, -1.0), gates - high)

    normed32 = normed.astype(F32)
    own_half = jnp.where(k == 0, normed32[:, :half], normed32[:, half:])
    zbuf[z] = jnp.concatenate([own_half, meta], axis=1).astype(BF16)
    z_copies = []
    for d in range(1, 8):
        copy = pltpu.make_async_remote_copy(
            src_ref=zbuf.at[z],
            dst_ref=zbuf.at[z],
            send_sem=z_send.at[d],
            recv_sem=z_recv.at[d],
            device_id=(z_peer(d), k),
            device_id_type=MESH,
        )
        copy.start()
        z_copies.append(copy)

    count = 8 * tokens
    slots = 128
    row = lax.broadcasted_iota(jnp.int32, (slots, 2 * experts), 0)
    col = lax.broadcasted_iota(jnp.int32, (slots, 2 * experts), 1)
    pick_high = jnp.where(col == 8 * z + row // 16, 1.0, 0.0).astype(BF16)
    pick_low = jnp.where(col == experts + 8 * z + row // 16, 1.0, 0.0).astype(BF16)
    row = lax.broadcasted_iota(jnp.int32, (count, count), 0)
    col = lax.broadcasted_iota(jnp.int32, (count, count), 1)
    same = row // tokens == col // tokens
    before = jnp.where(same & (row < col), 1.0, 0.0).astype(BF16)
    after = jnp.where(same & (col < row), 1.0, 0.0).astype(BF16)

    for copy in z_copies:
        copy.wait()
    gathered = zbuf[...].astype(F32).reshape(count, half + 2 * experts)
    metas = gathered[:, half:].astype(BF16)
    states = gathered[:, :half].astype(BF16)
    row = lax.broadcasted_iota(jnp.int32, (slots, count), 0)
    col = lax.broadcasted_iota(jnp.int32, (slots, count), 1)
    taken = jnp.where(dot_nt(pick_high, metas) >= 0, 1.0, 0.0)
    rank = dot_nn(taken.astype(BF16), before)
    hit = (taken > 0) & (col // tokens == (row // 2) % 8) & (rank == (row % 2).astype(F32))
    spread = dot_nn(jnp.where(hit, 1.0, 0.0).astype(BF16), states)
    psend[...] = spread.reshape(8, 16, half).astype(BF16)
    p_copies = []
    for i in range(1, 16):
        dev, pk, block = plane_peer(i)
        copy = pltpu.make_async_remote_copy(
            src_ref=psend.at[block],
            dst_ref=xbuf.at[core, k, line],
            send_sem=p_send.at[i],
            recv_sem=p_recv.at[i],
            device_id=(dev, pk),
            device_id_type=MESH,
        )
        copy.start()
        p_copies.append(copy)
    xbuf[core, k, line] = psend[line]

    row = lax.broadcasted_iota(jnp.int32, (count, slots), 0)
    col = lax.broadcasted_iota(jnp.int32, (count, slots), 1)
    gate_high = dot_nt(metas, pick_high)
    gate_low = dot_nt(metas, pick_low)
    taken = jnp.where(gate_high >= 0, 1.0, 0.0)
    rank = dot_nn(after, taken.astype(BF16))
    hit = (taken > 0) & (row // tokens == (col // 2) % 8) & (rank == (col % 2).astype(F32))
    combine_high = jnp.where(hit, gate_high, 0.0).astype(BF16)
    combine_low = jnp.where(hit, gate_low, 0.0).astype(BF16)

    s_copies = []
    for i in range(16):
        if i > 0:
            p_copies[i - 1].wait()
        sy = (y + 4 - i // 4) % 4
        sx = (xh + (i // 2) % 2) % 2
        sk = (k + i % 2) % 2
        copy = pltpu.make_async_remote_copy(
            src_ref=xbuf.at[core, sk, sy * 2 + sx],
            dst_ref=xbuf.at[core, sk, sy * 2 + sx],
            send_sem=s_send.at[i],
            recv_sem=s_recv.at[i],
            device_id=(sibling, k),
            device_id_type=MESH,
        )
        copy.start()
        s_copies.append(copy)
    for copy in w_loads:
        copy.wait()
    for copy in s_copies:
        copy.wait()

    def feed_forward(side):
        left = xbuf[side, 0].astype(F32).reshape(slots, half).astype(BF16)
        right = xbuf[side, 1].astype(F32).reshape(slots, half).astype(BF16)
        gate = dot_nt(left, gu[0, :, :half]) + dot_nt(right, gu[0, :, half:])
        up = dot_nt(left, gu[1, :, :half]) + dot_nt(right, gu[1, :, half:])
        activated = (gate / (1.0 + jnp.exp(-gate)) * up).astype(BF16)
        return dot_nn(activated, down[...])

    ysend[...] = feed_forward(1 - core).astype(BF16)
    trade = pltpu.make_async_remote_copy(
        src_ref=ysend,
        dst_ref=ybuf,
        send_sem=y_sem.at[0],
        recv_sem=y_sem.at[1],
        device_id=(sibling, k),
        device_id_type=MESH,
    )
    trade.start()
    own = feed_forward(core)
    trade.wait()
    both = own + ybuf[...].astype(F32)
    rsend[0] = both[:, :half].reshape(8, 16, half).astype(BF16)
    rsend[1] = both[:, half:].reshape(8, 16, half).astype(BF16)
    r_copies = []
    for i in range(1, 16):
        dev, pk, block = plane_peer(i)
        copy = pltpu.make_async_remote_copy(
            src_ref=rsend.at[pk, block],
            dst_ref=rbuf.at[k, line],
            send_sem=r_send.at[i],
            recv_sem=r_recv.at[i],
            device_id=(dev, pk),
            device_id_type=MESH,
        )
        copy.start()
        r_copies.append(copy)
    rbuf[k, line] = rsend[k, line]
    for copy in r_copies:
        copy.wait()
    routed = jnp.zeros((count, half), F32)
    for side in range(2):
        arrived = rbuf[side].astype(F32).reshape(slots, half).astype(BF16)
        routed += dot_nn(combine_high, arrived) + dot_nn(combine_low, arrived)
    csend[...] = routed.reshape(8, tokens, half).astype(BF16)
    c_copies = []
    for d in range(1, 8):
        copy = pltpu.make_async_remote_copy(
            src_ref=csend.at[(z + d) % 8],
            dst_ref=fbuf.at[z],
            send_sem=c_send.at[d],
            recv_sem=c_recv.at[d],
            device_id=(z_peer(d), k),
            device_id_type=MESH,
        )
        copy.start()
        c_copies.append(copy)
    fbuf[z] = csend[z]
    for copy in c_copies:
        copy.wait()
    total = jnp.sum(fbuf[...].astype(F32), axis=0)
    own_mixed = jnp.where(k == 0, mixed[:, :half], mixed[:, half:])
    mine = (own_mixed + total).astype(BF16)
    osend[...] = mine
    final = pltpu.make_async_remote_copy(
        src_ref=osend,
        dst_ref=obuf,
        send_sem=o_sem.at[0],
        recv_sem=o_sem.at[1],
        device_id=(me, 1 - k),
        device_id_type=MESH,
    )
    final.start()
    final.wait()
    mine32, other32 = mine.astype(F32), obuf[...].astype(F32)
    out_ref[:, :half] = jnp.where(k == 0, mine32, other32).astype(BF16)
    out_ref[:, half:] = jnp.where(k == 0, other32, mine32).astype(BF16)


def finish_kernel(hidden_ref, stat_ref, out_ref, norm_ref, logit_ref):
    out_ref[...] = hidden_ref[...]
    stats = stat_ref[...]
    row = lax.broadcasted_iota(jnp.int32, stats.shape, 0)
    col = lax.broadcasted_iota(jnp.int32, stats.shape, 1)
    for target, lane in ((norm_ref, 0), (logit_ref, 1)):
        column = jnp.broadcast_to(stats[:, lane : lane + 1], stats.shape)
        line = jnp.sum(jnp.where(row == col, column, 0.0), axis=0)
        target[...] = line[: target.shape[0]]


def to_rows(array):
    lead = math.prod(array.shape[:-2])
    head_dim = array.shape[-1] // 2
    split = array.reshape(lead, array.shape[-2], 2, head_dim)
    return split.transpose(0, 2, 1, 3).reshape(-1, head_dim)


def body(
    hidden,
    queries,
    fresh_key_value,
    kv_pool,
    page_table,
    lengths,
    out_weight,
    norm_gain,
    router_weight,
    expert_ids,
    expert_gate_up,
    expert_down,
):
    tokens, width = hidden.shape
    half = width // 2
    pages, page_len, kv_heads, pair = kv_pool.shape
    head_dim = pair // 2
    pool_rows = to_rows(kv_pool)
    fresh_rows = to_rows(fresh_key_value)
    rows = pool_rows.shape[0]
    heads = queries.shape[1] // head_dim
    page_rows = rows // pages
    vmem = pl.BlockSpec(memory_space=pltpu.VMEM)
    smem = pl.BlockSpec(memory_space=pltpu.SMEM)
    hbm = pl.BlockSpec(memory_space=pltpu.HBM)
    pool_new = pl.pallas_call(
        functools.partial(pool_kernel, page_len),
        out_shape=jax.ShapeDtypeStruct(pool_rows.shape, BF16),
        in_specs=[smem, smem, vmem, hbm],
        out_specs=hbm,
        scratch_shapes=[
            pltpu.VMEM(pool_rows.shape, BF16),
            pltpu.SemaphoreType.DMA((8,)),
            pltpu.SemaphoreType.DMA((8,)),
        ],
    )(page_table, lengths, fresh_rows, pool_rows)
    updated_pool = (
        pool_new.reshape(pages * page_len, 2, kv_heads, head_dim)
        .transpose(0, 2, 1, 3)
        .reshape(kv_pool.shape)
    )
    gate_up = expert_gate_up[0]
    down = expert_down[0]
    experts = router_weight.shape[0]
    dma = pltpu.SemaphoreType.DMA
    out_raw, stats = pl.pallas_call(
        functools.partial(expert_kernel, page_len),
        out_shape=(
            jax.ShapeDtypeStruct((tokens, width), BF16),
            jax.ShapeDtypeStruct((tokens, 2 * experts), F32),
        ),
        in_specs=[smem, vmem, vmem, vmem, vmem, vmem, vmem, hbm, hbm, hbm, hbm],
        out_specs=(vmem, vmem),
        scratch_shapes=[
            pltpu.VMEM(pool_rows.shape, BF16),
            pltpu.VMEM(out_weight.shape, BF16),
            pltpu.VMEM((pages, heads * tokens, page_rows), F32),
            pltpu.VMEM((pages, 2, tokens, page_rows), F32),
            pltpu.VMEM((tokens, width), BF16),
            pltpu.VMEM(gate_up.shape, BF16),
            pltpu.VMEM(down.shape, BF16),
            pltpu.VMEM((tokens, width), BF16),
            pltpu.VMEM((2 * experts, width), BF16),
            pltpu.VMEM((8, tokens, half + 2 * experts), BF16),
            pltpu.VMEM((8, 16, half), BF16),
            pltpu.VMEM((2, 2, 8, 16, half), BF16),
            pltpu.VMEM((128, width), BF16),
            pltpu.VMEM((128, width), BF16),
            pltpu.VMEM((2, 8, 16, half), BF16),
            pltpu.VMEM((2, 8, 16, half), BF16),
            pltpu.VMEM((8, tokens, half), BF16),
            pltpu.VMEM((8, tokens, half), BF16),
            pltpu.VMEM((tokens, half), BF16),
            pltpu.VMEM((tokens, half), BF16),
            dma((3,)),
            dma((2,)),
            dma((8,)),
            dma((8,)),
            dma((16,)),
            dma((16,)),
            dma((16,)),
            dma((16,)),
            dma((2,)),
            dma((16,)),
            dma((16,)),
            dma((8,)),
            dma((8,)),
            dma((2,)),
            dma((8,)),
            dma((4,)),
        ],
        compiler_params=pltpu.CompilerParams(collective_id=0, has_side_effects=True),
    )(
        lengths,
        page_table,
        queries,
        hidden,
        norm_gain,
        router_weight,
        expert_ids,
        pool_new,
        out_weight,
        gate_up,
        down,
    )
    out_hidden, norms, max_logit = pl.pallas_call(
        finish_kernel,
        out_shape=(
            jax.ShapeDtypeStruct((tokens, width), BF16),
            jax.ShapeDtypeStruct((tokens,), F32),
            jax.ShapeDtypeStruct((tokens,), F32),
        ),
        in_specs=[vmem, vmem],
        out_specs=(vmem, vmem, vmem),
    )(out_raw, stats)
    return (out_hidden, updated_pool, norms, max_logit)


def solution(mesh):
    in_specs = (
        P("req", None),
        P("req", "kv"),
        P("req", "kv", None),
        P("req", None, "kv", None),
        P("req", None),
        P("req"),
        P("kv", None),
        P(),
        P(),
        P("req", None),
        P("req", None, "kv", None),
        P("req", "kv", None),
    )
    out_specs = (P("req", None), P("req", None, "kv", None), P("req"), P("req"))
    return jax.shard_map(body, mesh=mesh, in_specs=in_specs, out_specs=out_specs, check_vma=False)
```

```python
import functools
import math

import jax
import jax.numpy as jnp
from jax import lax
from jax.experimental import pallas as pl
from jax.experimental.pallas import tpu as pltpu
from jax.sharding import PartitionSpec as P

MESH = pl.DeviceIdType.MESH
F32 = jnp.float32
BF16 = jnp.bfloat16


def dot_nn(a, b):
    return lax.dot_general(a, b, (((1,), (0,)), ((), ())), preferred_element_type=F32)


def dot_nt(a, b):
    return lax.dot_general(a, b, (((1,), (1,)), ((), ())), preferred_element_type=F32)


def pool_kernel(page_len, table_s, lens_s, fresh_ref, pool_hbm, pool_out, kv, in_sem, out_sem):
    reqs = table_s.shape[0]
    head_dim = kv.shape[1]
    chunks = in_sem.shape[0]
    chunk = kv.shape[0] // chunks
    loads = [
        pltpu.make_async_copy(
            pool_hbm.at[pl.ds(i * chunk, chunk)], kv.at[pl.ds(i * chunk, chunk)], in_sem.at[i]
        )
        for i in range(chunks)
    ]
    for copy in loads:
        copy.start()
    row = lax.broadcasted_iota(jnp.int32, (16, head_dim), 0)
    bases, news = [], []
    for r in range(reqs):
        length = lens_s[r]
        page = table_s[r, length // page_len]
        position = page * page_len + length % page_len
        bases.append(position // 4)
        four = fresh_ref[4 * r : 4 * r + 4, :].astype(F32)
        news.append((row // 4 == position % 4, jnp.concatenate([four, four, four, four], axis=0)))
    stores = []
    for i in range(chunks):
        loads[i].wait()
        for r in range(reqs):

            @pl.when(bases[r] // (chunk // 16) == i)
            def _():
                base = pl.multiple_of(bases[r] * 16, 16)
                hit, tiled = news[r]
                old = kv[pl.ds(base, 16), :].astype(F32)
                kv[pl.ds(base, 16), :] = jnp.where(hit, tiled, old).astype(BF16)

        copy = pltpu.make_async_copy(
            kv.at[pl.ds(i * chunk, chunk)], pool_out.at[pl.ds(i * chunk, chunk)], out_sem.at[i]
        )
        copy.start()
        stores.append(copy)
    for copy in stores:
        copy.wait()


def attend(page_len, table_v, lens_s, q_ref, kv, scores, weight, loads, ow_loads):
    reqs, max_pages = table_v.shape
    head_dim = kv.shape[1]
    page_rows = 4 * page_len
    pages = kv.shape[0] // page_rows
    req_row = lax.broadcasted_iota(jnp.int32, (reqs, page_rows), 0)
    lane = lax.broadcasted_iota(jnp.int32, (reqs, page_rows), 1)
    lens = jnp.zeros((reqs, page_rows), jnp.int32)
    for r in range(reqs):
        lens = jnp.where(req_row == r, lens_s[r], lens)
    last_page = lens // page_len
    rem = lens % page_len
    whole = jnp.zeros((reqs, page_rows), F32)
    partial = jnp.zeros((reqs, page_rows), F32)
    for j in range(max_pages):
        named = lane == table_v[:, j : j + 1]
        whole += jnp.where(named & (last_page > j), 1.0, 0.0)
        partial += jnp.where(named & (last_page == j), 1.0, 0.0)
    seen = (lane // 4) <= rem
    is_key = (lane % 4) < 2
    masks = []
    for head in range(2):
        mine = is_key & ((lane % 2) == head)
        masks.append((jnp.where(mine, 1.0, 0.0), jnp.where(mine & seen, 1.0, 0.0)))
    for p in range(pages):
        full = jnp.broadcast_to(whole[:, p : p + 1], (reqs, page_rows))
        part = jnp.broadcast_to(partial[:, p : p + 1], (reqs, page_rows))
        for head in range(2):
            weight[p, head] = full * masks[head][0] + part * masks[head][1]

    query = q_ref[...].astype(F32)
    heads = query.shape[1] // head_dim
    group = heads // 2
    stacked = jnp.concatenate(
        [query[:, h * head_dim : (h + 1) * head_dim] for h in range(heads)], axis=0
    ).astype(BF16)
    scale = 1.0 / math.sqrt(head_dim)
    groups = len(loads)
    span = pages // groups
    rows = span * page_rows

    def score_group(g, top):
        block = kv[pl.ds(pl.multiple_of(g * rows, rows), rows), :]
        s = dot_nt(stacked, block)
        tops = [top[h * reqs : (h + 1) * reqs, :] for h in range(heads)]
        for i in range(span):
            p = g * span + i
            for h in range(heads):
                w = weight[p, h // group]
                piece = s[h * reqs : (h + 1) * reqs, i * page_rows : (i + 1) * page_rows]
                masked = jnp.where(w > 0, piece, -1e30)
                scores[p, h * reqs : (h + 1) * reqs, :] = masked
                tops[h] = jnp.maximum(tops[h], masked)
        return jnp.concatenate(tops, axis=0)

    def value_group(g, carry):
        total, acc = carry
        parts = []
        for i in range(span):
            p = g * span + i
            w = jnp.concatenate([weight[p, h // group] for h in range(heads)], axis=0)
            e = jnp.exp((scores[p] - top) * scale) * w
            total += e
            parts.append(pltpu.roll(e, 2, 1).astype(BF16))
        block = kv[pl.ds(pl.multiple_of(g * rows, rows), rows), :]
        acc += dot_nn(jnp.concatenate(parts, axis=1), block)
        return total, acc

    top = jnp.full((heads * reqs, page_rows), -1e30, F32)
    for g in range(groups):
        loads[g].wait()
        top = score_group(g, top)
    for copy in ow_loads:
        copy.start()
    top = jnp.max(top, axis=1, keepdims=True)
    carry = (
        jnp.zeros((heads * reqs, page_rows), F32),
        jnp.zeros((heads * reqs, head_dim), F32),
    )
    for g in range(groups):
        carry = value_group(g, carry)
    total, acc = carry
    result = acc / jnp.sum(total, axis=1, keepdims=True)
    return jnp.concatenate(
        [result[h * reqs : (h + 1) * reqs, :] for h in range(heads)], axis=1
    ).astype(BF16)


Z_ORDER = (4, 3, 5, 2, 6, 1, 7)
PLANE_ORDER = (10, 8, 11, 9, 6, 14, 4, 12, 7, 15, 5, 13, 2, 3, 1)


def expert_kernel(
    page_len,
    lens_s,
    table_v,
    q_ref,
    hidden_ref,
    gain_ref,
    router_ref,
    ids_ref,
    pool_hbm,
    ow_hbm,
    gu_hbm,
    down_hbm,
    out_ref,
    stat_ref,
    kv,
    ow,
    scores,
    weight,
    part_ref,
    gu,
    down,
    pbuf,
    router2,
    zbuf,
    psend,
    xbuf,
    down2,
    asend,
    abuf,
    rsend,
    rbuf,
    csend,
    fbuf,
    w_sem,
    kv_sem,
    z_send,
    z_recv,
    p_send,
    p_recv,
    s_send,
    s_recv,
    y_sem,
    r_send,
    r_recv,
    c_send,
    c_recv,
    in_sem,
    ow_sem,
):
    me = lax.axis_index("req")
    k = lax.axis_index("kv")
    core = me % 2
    xh = (me // 2) % 2
    y = (me // 4) % 4
    z = me // 16
    line = y * 2 + xh
    sibling = me + 1 - 2 * core

    def plane_peer(i):
        py = (y + i // 4) % 4
        px = (xh + (i // 2) % 2) % 2
        pk = (k + i % 2) % 2
        return z * 16 + py * 4 + px * 2 + core, pk, py * 2 + px

    def z_peer(d):
        return ((z + d) % 8) * 16 + me % 16

    barrier = pltpu.get_barrier_semaphore()
    for i in range(1, 16):
        dev, pk, _ = plane_peer(i)
        pl.semaphore_signal(barrier, inc=1, device_id=(dev, pk), device_id_type=MESH)
    for d in range(1, 8):
        for side in range(2):
            pl.semaphore_signal(barrier, inc=1, device_id=(z_peer(d), side), device_id_type=MESH)
    pl.semaphore_signal(barrier, inc=1, device_id=(sibling, k), device_id_type=MESH)

    chunks = in_sem.shape[0]
    chunk = kv.shape[0] // chunks
    loads = [
        pltpu.make_async_copy(
            pool_hbm.at[pl.ds(i * chunk, chunk)], kv.at[pl.ds(i * chunk, chunk)], in_sem.at[i]
        )
        for i in range(chunks)
    ]
    ow_chunks = ow_sem.shape[0]
    ow_chunk = ow.shape[0] // ow_chunks
    ow_loads = [
        pltpu.make_async_copy(
            ow_hbm.at[pl.ds(i * ow_chunk, ow_chunk)],
            ow.at[pl.ds(i * ow_chunk, ow_chunk)],
            ow_sem.at[i],
        )
        for i in range(ow_chunks)
    ]
    w_loads = [
        pltpu.make_async_copy(gu_hbm.at[0], gu.at[0], w_sem.at[0]),
        pltpu.make_async_copy(gu_hbm.at[1], gu.at[1], w_sem.at[1]),
        pltpu.make_async_copy(down_hbm, down, w_sem.at[2]),
    ]
    for copy in loads:
        copy.start()
    attended = attend(page_len, table_v, lens_s, q_ref, kv, scores, weight, loads, ow_loads)
    for copy in ow_loads:
        copy.wait()
    for copy in w_loads:
        copy.start()
    part_ref[...] = dot_nn(attended, ow[...]).astype(BF16)
    pl.semaphore_wait(barrier, 30)

    swap = pltpu.make_async_remote_copy(
        src_ref=part_ref,
        dst_ref=pbuf,
        send_sem=kv_sem.at[0],
        recv_sem=kv_sem.at[1],
        device_id=(me, 1 - k),
        device_id_type=MESH,
    )
    swap.start()
    lend = pltpu.make_async_remote_copy(
        src_ref=down_hbm,
        dst_ref=down2,
        send_sem=y_sem.at[2],
        recv_sem=y_sem.at[3],
        device_id=(sibling, k),
        device_id_type=MESH,
    )
    lend.start()
    tokens, width = hidden_ref.shape
    half = width // 2
    experts = router_ref.shape[0]
    chosen_count = ids_ref.shape[1]
    router2[0:experts, :] = router_ref[...]
    router2[experts : 2 * experts, :] = router_ref[...]
    lane = lax.broadcasted_iota(jnp.int32, (tokens, 2 * experts), 1)
    chosen = jnp.zeros((tokens, 2 * experts), F32)
    for j in range(chosen_count):
        chosen += jnp.where(lane % experts == ids_ref[:, j : j + 1], 1.0, 0.0)
    swap.wait()
    projected = part_ref[...].astype(F32) + pbuf[...].astype(F32)
    mixed = (hidden_ref[...].astype(F32) + projected).astype(BF16).astype(F32)
    norms = jnp.sqrt(jnp.sum(mixed * mixed, axis=1, keepdims=True) / width + 1e-06)
    normed = (mixed / norms * gain_ref[...].astype(F32).reshape(1, width)).astype(BF16)
    logits = dot_nt(normed, router2[...])
    stat_ref[...] = jnp.where(
        lane == 0, norms, jnp.max(logits, axis=1, keepdims=True)
    )
    raised = jnp.where(chosen > 0, jnp.exp(logits), 0.0)
    gates = raised / jnp.sum(jnp.where(lane < experts, raised, 0.0), axis=1, keepdims=True)
    high = gates.astype(BF16).astype(F32)
    meta = jnp.where(lane < experts, jnp.where(chosen > 0, high, -1.0), gates - high)

    normed32 = normed.astype(F32)
    own_half = jnp.where(k == 0, normed32[:, :half], normed32[:, half:])
    zbuf[z] = jnp.concatenate([own_half, meta], axis=1).astype(BF16)
    z_copies = []
    for d in Z_ORDER:
        copy = pltpu.make_async_remote_copy(
            src_ref=zbuf.at[z],
            dst_ref=zbuf.at[z],
            send_sem=z_send.at[d],
            recv_sem=z_recv.at[d],
            device_id=(z_peer(d), k),
            device_id_type=MESH,
        )
        copy.start()
        z_copies.append(copy)

    count = 8 * tokens
    slots = 128
    row = lax.broadcasted_iota(jnp.int32, (slots, 2 * experts), 0)
    col = lax.broadcasted_iota(jnp.int32, (slots, 2 * experts), 1)
    pick_high = jnp.where(col == 8 * z + row // 16, 1.0, 0.0).astype(BF16)
    pick_low = jnp.where(col == experts + 8 * z + row // 16, 1.0, 0.0).astype(BF16)
    row = lax.broadcasted_iota(jnp.int32, (count, count), 0)
    col = lax.broadcasted_iota(jnp.int32, (count, count), 1)
    same = row // tokens == col // tokens
    before = jnp.where(same & (row < col), 1.0, 0.0).astype(BF16)
    after = jnp.where(same & (col < row), 1.0, 0.0).astype(BF16)

    for copy in z_copies:
        copy.wait_recv()
    gathered = zbuf[...].astype(F32).reshape(count, half + 2 * experts)
    metas = gathered[:, half:].astype(BF16)
    states = gathered[:, :half].astype(BF16)
    row = lax.broadcasted_iota(jnp.int32, (slots, count), 0)
    col = lax.broadcasted_iota(jnp.int32, (slots, count), 1)
    taken = jnp.where(dot_nt(pick_high, metas) >= 0, 1.0, 0.0)
    rank = dot_nn(taken.astype(BF16), before)
    hit = (taken > 0) & (col // tokens == (row // 2) % 8) & (rank == (row % 2).astype(F32))
    spread = dot_nn(jnp.where(hit, 1.0, 0.0).astype(BF16), states)
    psend[...] = spread.reshape(8, 16, half).astype(BF16)
    p_copies = {}
    for i in PLANE_ORDER:
        dev, pk, block = plane_peer(i)
        copy = pltpu.make_async_remote_copy(
            src_ref=psend.at[block],
            dst_ref=xbuf.at[core, k, line],
            send_sem=p_send.at[i],
            recv_sem=p_recv.at[i],
            device_id=(dev, pk),
            device_id_type=MESH,
        )
        copy.start()
        p_copies[i] = copy
    xbuf[core, k, line] = psend[line]

    row = lax.broadcasted_iota(jnp.int32, (count, slots), 0)
    col = lax.broadcasted_iota(jnp.int32, (count, slots), 1)
    gate_high = dot_nt(metas, pick_high)
    gate_low = dot_nt(metas, pick_low)
    taken = jnp.where(gate_high >= 0, 1.0, 0.0)
    rank = dot_nn(after, taken.astype(BF16))
    hit = (taken > 0) & (row // tokens == (col // 2) % 8) & (rank == (col % 2).astype(F32))
    combine_high = jnp.where(hit, gate_high, 0.0).astype(BF16)
    combine_low = jnp.where(hit, gate_low, 0.0).astype(BF16)

    s_copies = []
    for i in (0,) + PLANE_ORDER:
        if i > 0:
            p_copies[i].wait_recv()
        sy = (y + 4 - i // 4) % 4
        sx = (xh + (i // 2) % 2) % 2
        sk = (k + i % 2) % 2
        copy = pltpu.make_async_remote_copy(
            src_ref=xbuf.at[core, sk, sy * 2 + sx],
            dst_ref=xbuf.at[core, sk, sy * 2 + sx],
            send_sem=s_send.at[i],
            recv_sem=s_recv.at[i],
            device_id=(sibling, k),
            device_id_type=MESH,
        )
        copy.start()
        s_copies.append(copy)
    for copy in w_loads:
        copy.wait()

    def activate(side):
        left = xbuf[side, 0].astype(F32).reshape(slots, half).astype(BF16)
        right = xbuf[side, 1].astype(F32).reshape(slots, half).astype(BF16)
        gate = dot_nt(left, gu[0, :, :half]) + dot_nt(right, gu[0, :, half:])
        up = dot_nt(left, gu[1, :, :half]) + dot_nt(right, gu[1, :, half:])
        return (gate / (1.0 + jnp.exp(-gate)) * up).astype(BF16)

    activated = activate(core)
    for copy in s_copies:
        copy.wait_recv()
    asend[...] = activate(1 - core)
    trade = pltpu.make_async_remote_copy(
        src_ref=asend,
        dst_ref=abuf,
        send_sem=y_sem.at[0],
        recv_sem=y_sem.at[1],
        device_id=(sibling, k),
        device_id_type=MESH,
    )
    trade.start()
    own = dot_nn(activated, down[...])
    lend.wait_recv()
    trade.wait_recv()
    both = own + dot_nn(abuf[...], down2[...])
    rsend[0] = both[:, :half].reshape(8, 16, half).astype(BF16)
    rsend[1] = both[:, half:].reshape(8, 16, half).astype(BF16)
    r_copies = []
    for i in PLANE_ORDER:
        dev, pk, block = plane_peer(i)
        copy = pltpu.make_async_remote_copy(
            src_ref=rsend.at[pk, block],
            dst_ref=rbuf.at[k, line],
            send_sem=r_send.at[i],
            recv_sem=r_recv.at[i],
            device_id=(dev, pk),
            device_id_type=MESH,
        )
        copy.start()
        r_copies.append(copy)
    rbuf[k, line] = rsend[k, line]
    for copy in r_copies:
        copy.wait_recv()
    routed = jnp.zeros((count, half), F32)
    for side in range(2):
        arrived = rbuf[side].astype(F32).reshape(slots, half).astype(BF16)
        routed += dot_nn(combine_high, arrived) + dot_nn(combine_low, arrived)
    csend[...] = routed.reshape(8, tokens, half).astype(BF16)
    c_copies = []
    for j, d in enumerate(Z_ORDER + (0,)):
        for flip in (1, 0):
            if d + flip > 0:
                copy = pltpu.make_async_remote_copy(
                    src_ref=csend.at[(z + d) % 8],
                    dst_ref=fbuf.at[k, z],
                    send_sem=c_send.at[2 * j + flip],
                    recv_sem=c_recv.at[2 * j + flip],
                    device_id=(z_peer(d), (k + flip) % 2),
                    device_id_type=MESH,
                )
                copy.start()
                c_copies.append(copy)
    fbuf[k, z] = csend[z]
    for copy in c_copies:
        copy.wait_recv()
    for side in range(2):
        total = jnp.sum(fbuf[side].astype(F32), axis=0)
        part = mixed[:, side * half : (side + 1) * half]
        out_ref[:, side * half : (side + 1) * half] = (part + total).astype(BF16)
    for copy in z_copies + list(p_copies.values()) + s_copies + r_copies + c_copies:
        copy.wait_send()
    lend.wait_send()
    trade.wait_send()


def finish_kernel(hidden_ref, stat_ref, out_ref, norm_ref, logit_ref):
    out_ref[...] = hidden_ref[...]
    stats = stat_ref[...]
    row = lax.broadcasted_iota(jnp.int32, stats.shape, 0)
    col = lax.broadcasted_iota(jnp.int32, stats.shape, 1)
    for target, lane in ((norm_ref, 0), (logit_ref, 1)):
        column = jnp.broadcast_to(stats[:, lane : lane + 1], stats.shape)
        line = jnp.sum(jnp.where(row == col, column, 0.0), axis=0)
        target[...] = line[: target.shape[0]]


def to_rows(array):
    lead = math.prod(array.shape[:-2])
    head_dim = array.shape[-1] // 2
    split = array.reshape(lead, array.shape[-2], 2, head_dim)
    return split.transpose(0, 2, 1, 3).reshape(-1, head_dim)


def body(
    hidden,
    queries,
    fresh_key_value,
    kv_pool,
    page_table,
    lengths,
    out_weight,
    norm_gain,
    router_weight,
    expert_ids,
    expert_gate_up,
    expert_down,
):
    tokens, width = hidden.shape
    half = width // 2
    pages, page_len, kv_heads, pair = kv_pool.shape
    head_dim = pair // 2
    pool_rows = to_rows(kv_pool)
    fresh_rows = to_rows(fresh_key_value)
    rows = pool_rows.shape[0]
    heads = queries.shape[1] // head_dim
    page_rows = rows // pages
    vmem = pl.BlockSpec(memory_space=pltpu.VMEM)
    smem = pl.BlockSpec(memory_space=pltpu.SMEM)
    hbm = pl.BlockSpec(memory_space=pltpu.HBM)
    pool_new = pl.pallas_call(
        functools.partial(pool_kernel, page_len),
        out_shape=jax.ShapeDtypeStruct(pool_rows.shape, BF16),
        in_specs=[smem, smem, vmem, hbm],
        out_specs=hbm,
        scratch_shapes=[
            pltpu.VMEM(pool_rows.shape, BF16),
            pltpu.SemaphoreType.DMA((8,)),
            pltpu.SemaphoreType.DMA((8,)),
        ],
    )(page_table, lengths, fresh_rows, pool_rows)
    updated_pool = (
        pool_new.reshape(pages * page_len, 2, kv_heads, head_dim)
        .transpose(0, 2, 1, 3)
        .reshape(kv_pool.shape)
    )
    gate_up = expert_gate_up[0]
    down = expert_down[0]
    experts = router_weight.shape[0]
    dma = pltpu.SemaphoreType.DMA
    out_raw, stats = pl.pallas_call(
        functools.partial(expert_kernel, page_len),
        out_shape=(
            jax.ShapeDtypeStruct((tokens, width), BF16),
            jax.ShapeDtypeStruct((tokens, 2 * experts), F32),
        ),
        in_specs=[smem, vmem, vmem, vmem, vmem, vmem, vmem, hbm, hbm, hbm, hbm],
        out_specs=(vmem, vmem),
        scratch_shapes=[
            pltpu.VMEM(pool_rows.shape, BF16),
            pltpu.VMEM(out_weight.shape, BF16),
            pltpu.VMEM((pages, heads * tokens, page_rows), F32),
            pltpu.VMEM((pages, 2, tokens, page_rows), F32),
            pltpu.VMEM((tokens, width), BF16),
            pltpu.VMEM(gate_up.shape, BF16),
            pltpu.VMEM(down.shape, BF16),
            pltpu.VMEM((tokens, width), BF16),
            pltpu.VMEM((2 * experts, width), BF16),
            pltpu.VMEM((8, tokens, half + 2 * experts), BF16),
            pltpu.VMEM((8, 16, half), BF16),
            pltpu.VMEM((2, 2, 8, 16, half), BF16),
            pltpu.VMEM(down.shape, BF16),
            pltpu.VMEM((128, down.shape[0]), BF16),
            pltpu.VMEM((128, down.shape[0]), BF16),
            pltpu.VMEM((2, 8, 16, half), BF16),
            pltpu.VMEM((2, 8, 16, half), BF16),
            pltpu.VMEM((8, tokens, half), BF16),
            pltpu.VMEM((2, 8, tokens, half), BF16),
            dma((3,)),
            dma((2,)),
            dma((8,)),
            dma((8,)),
            dma((16,)),
            dma((16,)),
            dma((16,)),
            dma((16,)),
            dma((4,)),
            dma((16,)),
            dma((16,)),
            dma((16,)),
            dma((16,)),
            dma((13,)),
            dma((4,)),
        ],
        compiler_params=pltpu.CompilerParams(collective_id=0, has_side_effects=True),
    )(
        lengths,
        page_table,
        queries,
        hidden,
        norm_gain,
        router_weight,
        expert_ids,
        pool_new,
        out_weight,
        gate_up,
        down,
    )
    out_hidden, norms, max_logit = pl.pallas_call(
        finish_kernel,
        out_shape=(
            jax.ShapeDtypeStruct((tokens, width), BF16),
            jax.ShapeDtypeStruct((tokens,), F32),
            jax.ShapeDtypeStruct((tokens,), F32),
        ),
        in_specs=[vmem, vmem],
        out_specs=(vmem, vmem, vmem),
    )(out_raw, stats)
    return (out_hidden, updated_pool, norms, max_logit)


def solution(mesh):
    in_specs = (
        P("req", None),
        P("req", "kv"),
        P("req", "kv", None),
        P("req", None, "kv", None),
        P("req", None),
        P("req"),
        P("kv", None),
        P(),
        P(),
        P("req", None),
        P("req", None, "kv", None),
        P("req", "kv", None),
    )
    out_specs = (P("req", None), P("req", None, "kv", None), P("req"), P("req"))
    return jax.shard_map(body, mesh=mesh, in_specs=in_specs, out_specs=out_specs, check_vma=False)
```

```python
import functools
import math

import jax
import jax.numpy as jnp
from jax import lax
from jax.experimental import pallas as pl
from jax.experimental.pallas import tpu as pltpu
from jax.sharding import PartitionSpec as P

MESH = pl.DeviceIdType.MESH
F32 = jnp.float32
BF16 = jnp.bfloat16


def dot_nn(a, b):
    return lax.dot_general(a, b, (((1,), (0,)), ((), ())), preferred_element_type=F32)


def dot_nt(a, b):
    return lax.dot_general(a, b, (((1,), (1,)), ((), ())), preferred_element_type=F32)


def pool_kernel(
    page_len,
    table_hbm,
    lens_hbm,
    fresh_hbm,
    pool_hbm,
    pool_out,
    table_s,
    lens_s,
    fresh_ref,
    kv,
    in_sem,
    out_sem,
    small_sem,
):
    reqs = table_s.shape[0]
    small = [
        pltpu.make_async_copy(source, target, small_sem.at[i])
        for i, (source, target) in enumerate(
            ((table_hbm, table_s), (lens_hbm, lens_s), (fresh_hbm, fresh_ref))
        )
    ]
    for copy in small:
        copy.start()
    head_dim = kv.shape[1]
    chunks = in_sem.shape[0]
    chunk = kv.shape[0] // chunks
    loads = [
        pltpu.make_async_copy(
            pool_hbm.at[pl.ds(i * chunk, chunk)], kv.at[pl.ds(i * chunk, chunk)], in_sem.at[i]
        )
        for i in range(chunks)
    ]
    for copy in loads:
        copy.start()
    row = lax.broadcasted_iota(jnp.int32, (16, head_dim), 0)
    bases, news = [], []
    for copy in small:
        copy.wait()
    for r in range(reqs):
        length = lens_s[r]
        page = table_s[r, length // page_len]
        position = page * page_len + length % page_len
        bases.append(position // 4)
        four = fresh_ref[4 * r : 4 * r + 4, :].astype(F32)
        news.append((row // 4 == position % 4, jnp.concatenate([four, four, four, four], axis=0)))
    stores = []
    for i in range(chunks):
        loads[i].wait()
        for r in range(reqs):

            @pl.when(bases[r] // (chunk // 16) == i)
            def _():
                base = pl.multiple_of(bases[r] * 16, 16)
                hit, tiled = news[r]
                old = kv[pl.ds(base, 16), :].astype(F32)
                kv[pl.ds(base, 16), :] = jnp.where(hit, tiled, old).astype(BF16)

        copy = pltpu.make_async_copy(
            kv.at[pl.ds(i * chunk, chunk)], pool_out.at[pl.ds(i * chunk, chunk)], out_sem.at[i]
        )
        copy.start()
        stores.append(copy)
    for copy in stores:
        copy.wait()


def attend(page_len, table_v, lens_s, q_ref, kv, scores, weight, loads):
    reqs, max_pages = table_v.shape
    head_dim = kv.shape[1]
    page_rows = 4 * page_len
    pages = kv.shape[0] // page_rows
    req_row = lax.broadcasted_iota(jnp.int32, (reqs, page_rows), 0)
    lane = lax.broadcasted_iota(jnp.int32, (reqs, page_rows), 1)
    lens = jnp.zeros((reqs, page_rows), jnp.int32)
    for r in range(reqs):
        lens = jnp.where(req_row == r, lens_s[r], lens)
    last_page = lens // page_len
    rem = lens % page_len
    whole = jnp.zeros((reqs, page_rows), F32)
    partial = jnp.zeros((reqs, page_rows), F32)
    for j in range(max_pages):
        named = lane == table_v[:, j : j + 1]
        whole += jnp.where(named & (last_page > j), 1.0, 0.0)
        partial += jnp.where(named & (last_page == j), 1.0, 0.0)
    seen = (lane // 4) <= rem
    is_key = (lane % 4) < 2
    masks = []
    for head in range(2):
        mine = is_key & ((lane % 2) == head)
        masks.append((jnp.where(mine, 1.0, 0.0), jnp.where(mine & seen, 1.0, 0.0)))
    for p in range(pages):
        full = jnp.broadcast_to(whole[:, p : p + 1], (reqs, page_rows))
        part = jnp.broadcast_to(partial[:, p : p + 1], (reqs, page_rows))
        for head in range(2):
            weight[p, head] = full * masks[head][0] + part * masks[head][1]

    query = q_ref[...].astype(F32)
    heads = query.shape[1] // head_dim
    group = heads // 2
    stacked = jnp.concatenate(
        [query[:, h * head_dim : (h + 1) * head_dim] for h in range(heads)], axis=0
    ).astype(BF16)
    scale = 1.0 / math.sqrt(head_dim)
    groups = len(loads)
    span = pages // groups
    rows = span * page_rows

    def score_group(g, top):
        block = kv[pl.ds(pl.multiple_of(g * rows, rows), rows), :]
        s = dot_nt(stacked, block)
        tops = [top[h * reqs : (h + 1) * reqs, :] for h in range(heads)]
        for i in range(span):
            p = g * span + i
            for h in range(heads):
                w = weight[p, h // group]
                piece = s[h * reqs : (h + 1) * reqs, i * page_rows : (i + 1) * page_rows]
                masked = jnp.where(w > 0, piece, -1e30)
                scores[p, h * reqs : (h + 1) * reqs, :] = masked
                tops[h] = jnp.maximum(tops[h], masked)
        return jnp.concatenate(tops, axis=0)

    def value_group(g, carry):
        total, acc = carry
        parts = []
        for i in range(span):
            p = g * span + i
            w = jnp.concatenate([weight[p, h // group] for h in range(heads)], axis=0)
            e = jnp.exp((scores[p] - top) * scale) * w
            total += e
            parts.append(pltpu.roll(e, 2, 1).astype(BF16))
        block = kv[pl.ds(pl.multiple_of(g * rows, rows), rows), :]
        acc += dot_nn(jnp.concatenate(parts, axis=1), block)
        return total, acc

    top = jnp.full((heads * reqs, page_rows), -1e30, F32)
    for g in range(groups):
        loads[g].wait()
        top = score_group(g, top)
    top = jnp.max(top, axis=1, keepdims=True)
    carry = (
        jnp.zeros((heads * reqs, page_rows), F32),
        jnp.zeros((heads * reqs, head_dim), F32),
    )
    for g in range(groups):
        carry = value_group(g, carry)
    total, acc = carry
    result = acc / jnp.sum(total, axis=1, keepdims=True)
    return jnp.concatenate(
        [result[h * reqs : (h + 1) * reqs, :] for h in range(heads)], axis=1
    ).astype(BF16)


Z_ORDER = (4, 3, 5, 2, 6, 1, 7)
PLANE_ORDER = (10, 8, 11, 9, 6, 14, 4, 12, 7, 15, 5, 13, 2, 3, 1)


def expert_kernel(
    page_len,
    lens_hbm,
    table_hbm,
    q_hbm,
    hidden_hbm,
    gain_hbm,
    router_hbm,
    ids_hbm,
    pool_hbm,
    ow_hbm,
    gu_hbm,
    down_hbm,
    out_ref,
    stat_ref,
    lens_s,
    table_v,
    q_ref,
    hidden_ref,
    gain_ref,
    ids_ref,
    kv,
    ow,
    scores,
    weight,
    part_ref,
    gu,
    down,
    pbuf,
    router2,
    zbuf,
    zbuf2,
    psend,
    xbuf,
    down2,
    asend,
    abuf,
    rsend,
    rbuf,
    csend,
    fbuf,
    w_sem,
    kv_sem,
    z_send,
    z_recv,
    p_send,
    p_recv,
    s_send,
    s_recv,
    y_sem,
    r_send,
    r_recv,
    c_send,
    c_recv,
    in_sem,
    ow_sem,
    small_sem,
):
    me = lax.axis_index("req")
    k = lax.axis_index("kv")
    core = me % 2
    xh = (me // 2) % 2
    y = (me // 4) % 4
    z = me // 16
    line = y * 2 + xh
    sibling = me + 1 - 2 * core

    def plane_peer(i):
        py = (y + i // 4) % 4
        px = (xh + (i // 2) % 2) % 2
        pk = (k + i % 2) % 2
        return z * 16 + py * 4 + px * 2 + core, pk, py * 2 + px

    def z_peer(d):
        return ((z + d) % 8) * 16 + me % 16

    experts = router_hbm.shape[0]
    small = [
        pltpu.make_async_copy(source, target, small_sem.at[i])
        for i, (source, target) in enumerate(
            (
                (lens_hbm, lens_s),
                (table_hbm, table_v),
                (q_hbm, q_ref),
                (ids_hbm, ids_ref),
                (hidden_hbm, hidden_ref),
                (gain_hbm, gain_ref),
                (router_hbm, router2.at[pl.ds(0, experts)]),
                (router_hbm, router2.at[pl.ds(experts, experts)]),
            )
        )
    ]
    for copy in small[:3]:
        copy.start()
    barrier = pltpu.get_barrier_semaphore()
    for i in range(1, 16):
        dev, pk, _ = plane_peer(i)
        pl.semaphore_signal(barrier, inc=1, device_id=(dev, pk), device_id_type=MESH)
    for d in range(1, 8):
        for side in range(2):
            pl.semaphore_signal(barrier, inc=1, device_id=(z_peer(d), side), device_id_type=MESH)
    pl.semaphore_signal(barrier, inc=1, device_id=(sibling, k), device_id_type=MESH)

    chunks = in_sem.shape[0]
    chunk = kv.shape[0] // chunks
    loads = [
        pltpu.make_async_copy(
            pool_hbm.at[pl.ds(i * chunk, chunk)], kv.at[pl.ds(i * chunk, chunk)], in_sem.at[i]
        )
        for i in range(chunks)
    ]
    ow_chunks = ow_sem.shape[0]
    ow_chunk = ow.shape[0] // ow_chunks
    ow_loads = [
        pltpu.make_async_copy(
            ow_hbm.at[pl.ds(i * ow_chunk, ow_chunk)],
            ow.at[pl.ds(i * ow_chunk, ow_chunk)],
            ow_sem.at[i],
        )
        for i in range(ow_chunks)
    ]
    w_loads = [
        pltpu.make_async_copy(gu_hbm.at[0], gu.at[0], w_sem.at[0]),
        pltpu.make_async_copy(gu_hbm.at[1], gu.at[1], w_sem.at[1]),
        pltpu.make_async_copy(down_hbm, down, w_sem.at[2]),
    ]
    for copy in loads + ow_loads + small[3:]:
        copy.start()
    for copy in small[:3]:
        copy.wait()
    attended = attend(page_len, table_v, lens_s, q_ref, kv, scores, weight, loads)
    for copy in small[3:]:
        copy.wait()
    for copy in ow_loads:
        copy.wait()
    for copy in w_loads:
        copy.start()
    part_ref[...] = dot_nn(attended, ow[...]).astype(BF16)
    pl.semaphore_wait(barrier, 30)

    swap = pltpu.make_async_remote_copy(
        src_ref=part_ref,
        dst_ref=pbuf,
        send_sem=kv_sem.at[0],
        recv_sem=kv_sem.at[1],
        device_id=(me, 1 - k),
        device_id_type=MESH,
    )
    swap.start()
    lend = pltpu.make_async_remote_copy(
        src_ref=down_hbm,
        dst_ref=down2,
        send_sem=y_sem.at[2],
        recv_sem=y_sem.at[3],
        device_id=(sibling, k),
        device_id_type=MESH,
    )
    lend.start()
    tokens, width = hidden_ref.shape
    half = width // 2
    chosen_count = ids_ref.shape[1]
    lane = lax.broadcasted_iota(jnp.int32, (tokens, 2 * experts), 1)
    chosen = jnp.zeros((tokens, 2 * experts), F32)
    for j in range(chosen_count):
        chosen += jnp.where(lane % experts == ids_ref[:, j : j + 1], 1.0, 0.0)
    swap.wait()
    projected = part_ref[...].astype(F32) + pbuf[...].astype(F32)
    mixed = (hidden_ref[...].astype(F32) + projected).astype(BF16).astype(F32)
    norms = jnp.sqrt(jnp.sum(mixed * mixed, axis=1, keepdims=True) / width + 1e-06)
    normed = (mixed / norms * gain_ref[...].astype(F32).reshape(1, width)).astype(BF16)
    logits = dot_nt(normed, router2[...])
    stat_ref[...] = jnp.where(
        lane == 0, norms, jnp.max(logits, axis=1, keepdims=True)
    )
    raised = jnp.where(chosen > 0, jnp.exp(logits), 0.0)
    gates = raised / jnp.sum(jnp.where(lane < experts, raised, 0.0), axis=1, keepdims=True)
    high = gates.astype(BF16).astype(F32)
    meta = jnp.where(lane < experts, jnp.where(chosen > 0, high, -1.0), gates - high)

    normed32 = normed.astype(F32)
    own_half = jnp.where(k == 0, normed32[:, :half], normed32[:, half:])
    part_width = half // 2
    zbuf[z] = jnp.concatenate([own_half[:, :part_width], meta], axis=1).astype(BF16)
    zbuf2[z] = own_half[:, part_width:].astype(BF16)
    z_copies = []
    for q, buffer in enumerate((zbuf, zbuf2)):
        for d in Z_ORDER:
            copy = pltpu.make_async_remote_copy(
                src_ref=buffer.at[z],
                dst_ref=buffer.at[z],
                send_sem=z_send.at[8 * q + d],
                recv_sem=z_recv.at[8 * q + d],
                device_id=(z_peer(d), k),
                device_id_type=MESH,
            )
            copy.start()
            z_copies.append(copy)

    count = 8 * tokens
    slots = 128
    row = lax.broadcasted_iota(jnp.int32, (slots, 2 * experts), 0)
    col = lax.broadcasted_iota(jnp.int32, (slots, 2 * experts), 1)
    pick_high = jnp.where(col == 8 * z + row // 16, 1.0, 0.0).astype(BF16)
    pick_low = jnp.where(col == experts + 8 * z + row // 16, 1.0, 0.0).astype(BF16)
    row = lax.broadcasted_iota(jnp.int32, (count, count), 0)
    col = lax.broadcasted_iota(jnp.int32, (count, count), 1)
    same = row // tokens == col // tokens
    before = jnp.where(same & (row < col), 1.0, 0.0).astype(BF16)
    after = jnp.where(same & (col < row), 1.0, 0.0).astype(BF16)

    for copy in z_copies[:7]:
        copy.wait_recv()
    gathered = zbuf[...].astype(F32).reshape(count, part_width + 2 * experts)
    metas = gathered[:, part_width:].astype(BF16)
    row = lax.broadcasted_iota(jnp.int32, (slots, count), 0)
    col = lax.broadcasted_iota(jnp.int32, (slots, count), 1)
    taken = jnp.where(dot_nt(pick_high, metas) >= 0, 1.0, 0.0)
    rank = dot_nn(taken.astype(BF16), before)
    hit = (taken > 0) & (col // tokens == (row // 2) % 8) & (rank == (row % 2).astype(F32))
    dispatch = jnp.where(hit, 1.0, 0.0).astype(BF16)
    p_copies = {}
    for q in range(2):
        if q == 0:
            states = gathered[:, :part_width].astype(BF16)
        else:
            for copy in z_copies[7:]:
                copy.wait_recv()
            states = zbuf2[...].astype(F32).reshape(count, part_width).astype(BF16)
        psend[q] = dot_nn(dispatch, states).reshape(8, 16, part_width).astype(BF16)
        for i in PLANE_ORDER:
            dev, pk, block = plane_peer(i)
            copy = pltpu.make_async_remote_copy(
                src_ref=psend.at[q, block],
                dst_ref=xbuf.at[core, k, q, line],
                send_sem=p_send.at[16 * q + i],
                recv_sem=p_recv.at[16 * q + i],
                device_id=(dev, pk),
                device_id_type=MESH,
            )
            copy.start()
            p_copies[16 * q + i] = copy
        xbuf[core, k, q, line] = psend[q, line]

    row = lax.broadcasted_iota(jnp.int32, (count, slots), 0)
    col = lax.broadcasted_iota(jnp.int32, (count, slots), 1)
    gate_high = dot_nt(metas, pick_high)
    gate_low = dot_nt(metas, pick_low)
    taken = jnp.where(gate_high >= 0, 1.0, 0.0)
    rank = dot_nn(after, taken.astype(BF16))
    hit = (taken > 0) & (row // tokens == (col // 2) % 8) & (rank == (col % 2).astype(F32))
    combine_high = jnp.where(hit, gate_high, 0.0).astype(BF16)
    combine_low = jnp.where(hit, gate_low, 0.0).astype(BF16)

    s_copies = []
    for q in range(2):
        for i in (0,) + PLANE_ORDER:
            if i > 0:
                p_copies[16 * q + i].wait_recv()
            sy = (y + 4 - i // 4) % 4
            sx = (xh + (i // 2) % 2) % 2
            sk = (k + i % 2) % 2
            copy = pltpu.make_async_remote_copy(
                src_ref=xbuf.at[core, sk, q, sy * 2 + sx],
                dst_ref=xbuf.at[core, sk, q, sy * 2 + sx],
                send_sem=s_send.at[16 * q + i],
                recv_sem=s_recv.at[16 * q + i],
                device_id=(sibling, k),
                device_id_type=MESH,
            )
            copy.start()
            s_copies.append(copy)
    for copy in w_loads:
        copy.wait()

    def activate(side):
        gate = jnp.zeros((slots, down.shape[0]), F32)
        up = jnp.zeros((slots, down.shape[0]), F32)
        for q in range(2):
            for part in range(2):
                block = xbuf[side, part, q].astype(F32).reshape(slots, part_width).astype(BF16)
                first = part * half + q * part_width
                gate += dot_nt(block, gu[0, :, first : first + part_width])
                up += dot_nt(block, gu[1, :, first : first + part_width])
        return (gate / (1.0 + jnp.exp(-gate)) * up).astype(BF16)

    activated = activate(core)
    for copy in s_copies:
        copy.wait_recv()
    asend[...] = activate(1 - core)
    trade = pltpu.make_async_remote_copy(
        src_ref=asend,
        dst_ref=abuf,
        send_sem=y_sem.at[0],
        recv_sem=y_sem.at[1],
        device_id=(sibling, k),
        device_id_type=MESH,
    )
    trade.start()
    own = dot_nn(activated, down[...])
    lend.wait_recv()
    trade.wait_recv()
    arrived = abuf[...]
    r_copies = []
    for q in range(2):
        for part in range(2):
            first = part * half + q * part_width
            last = first + part_width
            both = own[:, first:last] + dot_nn(arrived, down2[:, first:last])
            rsend[q, part] = both.reshape(8, 16, part_width).astype(BF16)
        for i in PLANE_ORDER:
            dev, pk, block = plane_peer(i)
            copy = pltpu.make_async_remote_copy(
                src_ref=rsend.at[q, pk, block],
                dst_ref=rbuf.at[q, k, line],
                send_sem=r_send.at[16 * q + i],
                recv_sem=r_recv.at[16 * q + i],
                device_id=(dev, pk),
                device_id_type=MESH,
            )
            copy.start()
            r_copies.append(copy)
        rbuf[q, k, line] = rsend[q, k, line]
    c_copies = []
    for q in range(2):
        for copy in r_copies[15 * q : 15 * q + 15]:
            copy.wait_recv()
        routed = jnp.zeros((count, part_width), F32)
        for side in range(2):
            block = rbuf[q, side].astype(F32).reshape(slots, part_width).astype(BF16)
            routed += dot_nn(combine_high, block) + dot_nn(combine_low, block)
        csend[q] = routed.reshape(8, tokens, part_width).astype(BF16)
        for j, d in enumerate(Z_ORDER + (0,)):
            for flip in (1, 0):
                if d + flip > 0:
                    copy = pltpu.make_async_remote_copy(
                        src_ref=csend.at[q, (z + d) % 8],
                        dst_ref=fbuf.at[q, k, z],
                        send_sem=c_send.at[16 * q + 2 * j + flip],
                        recv_sem=c_recv.at[16 * q + 2 * j + flip],
                        device_id=(z_peer(d), (k + flip) % 2),
                        device_id_type=MESH,
                    )
                    copy.start()
                    c_copies.append(copy)
        fbuf[q, k, z] = csend[q, z]
    for q in range(2):
        for copy in c_copies[15 * q : 15 * q + 15]:
            copy.wait_recv()
        for side in range(2):
            total = jnp.sum(fbuf[q, side].astype(F32), axis=0)
            first = side * half + q * part_width
            last = first + part_width
            out_ref[:, first:last] = (mixed[:, first:last] + total).astype(BF16)
    for copy in z_copies + list(p_copies.values()) + s_copies + r_copies + c_copies:
        copy.wait_send()
    lend.wait_send()
    trade.wait_send()


def finish_kernel(hidden_ref, stat_ref, out_ref, norm_ref, logit_ref):
    out_ref[...] = hidden_ref[...]
    stats = stat_ref[...]
    row = lax.broadcasted_iota(jnp.int32, stats.shape, 0)
    col = lax.broadcasted_iota(jnp.int32, stats.shape, 1)
    for target, lane in ((norm_ref, 0), (logit_ref, 1)):
        column = jnp.broadcast_to(stats[:, lane : lane + 1], stats.shape)
        line = jnp.sum(jnp.where(row == col, column, 0.0), axis=0)
        target[...] = line[: target.shape[0]]


def to_rows(array):
    lead = math.prod(array.shape[:-2])
    head_dim = array.shape[-1] // 2
    split = array.reshape(lead, array.shape[-2], 2, head_dim)
    return split.transpose(0, 2, 1, 3).reshape(-1, head_dim)


def body(
    hidden,
    queries,
    fresh_key_value,
    kv_pool,
    page_table,
    lengths,
    out_weight,
    norm_gain,
    router_weight,
    expert_ids,
    expert_gate_up,
    expert_down,
):
    tokens, width = hidden.shape
    half = width // 2
    pages, page_len, kv_heads, pair = kv_pool.shape
    head_dim = pair // 2
    pool_rows = to_rows(kv_pool)
    fresh_rows = to_rows(fresh_key_value)
    rows = pool_rows.shape[0]
    heads = queries.shape[1] // head_dim
    page_rows = rows // pages
    vmem = pl.BlockSpec(memory_space=pltpu.VMEM)
    hbm = pl.BlockSpec(memory_space=pltpu.HBM)
    pool_new = pl.pallas_call(
        functools.partial(pool_kernel, page_len),
        out_shape=jax.ShapeDtypeStruct(pool_rows.shape, BF16),
        in_specs=[hbm, hbm, hbm, hbm],
        out_specs=hbm,
        scratch_shapes=[
            pltpu.SMEM(page_table.shape, jnp.int32),
            pltpu.SMEM(lengths.shape, jnp.int32),
            pltpu.VMEM(fresh_rows.shape, BF16),
            pltpu.VMEM(pool_rows.shape, BF16),
            pltpu.SemaphoreType.DMA((8,)),
            pltpu.SemaphoreType.DMA((8,)),
            pltpu.SemaphoreType.DMA((3,)),
        ],
    )(page_table, lengths, fresh_rows, pool_rows)
    updated_pool = (
        pool_new.reshape(pages * page_len, 2, kv_heads, head_dim)
        .transpose(0, 2, 1, 3)
        .reshape(kv_pool.shape)
    )
    gate_up = expert_gate_up[0]
    down = expert_down[0]
    experts = router_weight.shape[0]
    dma = pltpu.SemaphoreType.DMA
    out_raw, stats = pl.pallas_call(
        functools.partial(expert_kernel, page_len),
        out_shape=(
            jax.ShapeDtypeStruct((tokens, width), BF16),
            jax.ShapeDtypeStruct((tokens, 2 * experts), F32),
        ),
        in_specs=[hbm] * 11,
        out_specs=(vmem, vmem),
        scratch_shapes=[
            pltpu.SMEM(lengths.shape, jnp.int32),
            pltpu.VMEM(page_table.shape, jnp.int32),
            pltpu.VMEM(queries.shape, BF16),
            pltpu.VMEM(hidden.shape, BF16),
            pltpu.VMEM(norm_gain.shape, BF16),
            pltpu.VMEM(expert_ids.shape, jnp.int32),
            pltpu.VMEM(pool_rows.shape, BF16),
            pltpu.VMEM(out_weight.shape, BF16),
            pltpu.VMEM((pages, heads * tokens, page_rows), F32),
            pltpu.VMEM((pages, 2, tokens, page_rows), F32),
            pltpu.VMEM((tokens, width), BF16),
            pltpu.VMEM(gate_up.shape, BF16),
            pltpu.VMEM(down.shape, BF16),
            pltpu.VMEM((tokens, width), BF16),
            pltpu.VMEM((2 * experts, width), BF16),
            pltpu.VMEM((8, tokens, half // 2 + 2 * experts), BF16),
            pltpu.VMEM((8, tokens, half // 2), BF16),
            pltpu.VMEM((2, 8, 16, half // 2), BF16),
            pltpu.VMEM((2, 2, 2, 8, 16, half // 2), BF16),
            pltpu.VMEM(down.shape, BF16),
            pltpu.VMEM((128, down.shape[0]), BF16),
            pltpu.VMEM((128, down.shape[0]), BF16),
            pltpu.VMEM((2, 2, 8, 16, half // 2), BF16),
            pltpu.VMEM((2, 2, 8, 16, half // 2), BF16),
            pltpu.VMEM((2, 8, tokens, half // 2), BF16),
            pltpu.VMEM((2, 2, 8, tokens, half // 2), BF16),
            dma((3,)),
            dma((2,)),
            dma((16,)),
            dma((16,)),
            dma((32,)),
            dma((32,)),
            dma((32,)),
            dma((32,)),
            dma((4,)),
            dma((32,)),
            dma((32,)),
            dma((32,)),
            dma((32,)),
            dma((13,)),
            dma((4,)),
            dma((8,)),
        ],
        compiler_params=pltpu.CompilerParams(collective_id=0, has_side_effects=True),
    )(
        lengths,
        page_table,
        queries,
        hidden,
        norm_gain,
        router_weight,
        expert_ids,
        pool_new,
        out_weight,
        gate_up,
        down,
    )
    out_hidden, norms, max_logit = pl.pallas_call(
        finish_kernel,
        out_shape=(
            jax.ShapeDtypeStruct((tokens, width), BF16),
            jax.ShapeDtypeStruct((tokens,), F32),
            jax.ShapeDtypeStruct((tokens,), F32),
        ),
        in_specs=[vmem, vmem],
        out_specs=(vmem, vmem, vmem),
    )(out_raw, stats)
    return (out_hidden, updated_pool, norms, max_logit)


def solution(mesh):
    in_specs = (
        P("req", None),
        P("req", "kv"),
        P("req", "kv", None),
        P("req", None, "kv", None),
        P("req", None),
        P("req"),
        P("kv", None),
        P(),
        P(),
        P("req", None),
        P("req", None, "kv", None),
        P("req", "kv", None),
    )
    out_specs = (P("req", None), P("req", None, "kv", None), P("req"), P("req"))
    return jax.shard_map(body, mesh=mesh, in_specs=in_specs, out_specs=out_specs, check_vma=False)
```

```python
import functools
import math

import jax
import jax.numpy as jnp
from jax import lax
from jax.experimental import pallas as pl
from jax.experimental.pallas import tpu as pltpu
from jax.sharding import PartitionSpec as P

MESH = pl.DeviceIdType.MESH
F32 = jnp.float32
BF16 = jnp.bfloat16


def dot_nn(a, b):
    return lax.dot_general(a, b, (((1,), (0,)), ((), ())), preferred_element_type=F32)


def dot_nt(a, b):
    return lax.dot_general(a, b, (((1,), (1,)), ((), ())), preferred_element_type=F32)


def pool_kernel(
    page_len,
    table_hbm,
    lens_hbm,
    fresh_hbm,
    pool_hbm,
    pool_out,
    table_s,
    lens_s,
    fresh_ref,
    kv,
    in_sem,
    out_sem,
    small_sem,
):
    reqs = table_s.shape[0]
    head_dim = kv.shape[1]
    chunks = in_sem.shape[0]
    chunk = kv.shape[0] // chunks
    loads = [
        pltpu.make_async_copy(
            pool_hbm.at[pl.ds(i * chunk, chunk)], kv.at[pl.ds(i * chunk, chunk)], in_sem.at[i]
        )
        for i in range(chunks)
    ]
    small = [
        pltpu.make_async_copy(source, target, small_sem.at[i])
        for i, (source, target) in enumerate(
            ((table_hbm, table_s), (lens_hbm, lens_s), (fresh_hbm, fresh_ref))
        )
    ]
    for copy in small + loads:
        copy.start()
    row = lax.broadcasted_iota(jnp.int32, (16, head_dim), 0)
    bases, news = [], []
    for copy in small:
        copy.wait()
    for r in range(reqs):
        length = lens_s[r]
        page = table_s[r, length // page_len]
        position = page * page_len + length % page_len
        bases.append(position // 4)
        four = fresh_ref[4 * r : 4 * r + 4, :].astype(F32)
        news.append((row // 4 == position % 4, jnp.concatenate([four, four, four, four], axis=0)))
    stores = []
    for i in range(chunks):
        loads[i].wait()
        for r in range(reqs):

            @pl.when(bases[r] // (chunk // 16) == i)
            def _():
                base = pl.multiple_of(bases[r] * 16, 16)
                hit, tiled = news[r]
                old = kv[pl.ds(base, 16), :].astype(F32)
                kv[pl.ds(base, 16), :] = jnp.where(hit, tiled, old).astype(BF16)

        copy = pltpu.make_async_copy(
            kv.at[pl.ds(i * chunk, chunk)], pool_out.at[pl.ds(i * chunk, chunk)], out_sem.at[i]
        )
        copy.start()
        stores.append(copy)
    for copy in stores:
        copy.wait()


def attend(page_len, table_v, lens_s, q_ref, kv, scores, weight, loads):
    reqs, max_pages = table_v.shape
    head_dim = kv.shape[1]
    page_rows = 4 * page_len
    pages = kv.shape[0] // page_rows
    req_row = lax.broadcasted_iota(jnp.int32, (reqs, page_rows), 0)
    lane = lax.broadcasted_iota(jnp.int32, (reqs, page_rows), 1)
    lens = jnp.zeros((reqs, page_rows), jnp.int32)
    for r in range(reqs):
        lens = jnp.where(req_row == r, lens_s[r], lens)
    last_page = lens // page_len
    rem = lens % page_len
    whole = jnp.zeros((reqs, page_rows), F32)
    partial = jnp.zeros((reqs, page_rows), F32)
    for j in range(max_pages):
        named = lane == table_v[:, j : j + 1]
        whole += jnp.where(named & (last_page > j), 1.0, 0.0)
        partial += jnp.where(named & (last_page == j), 1.0, 0.0)
    seen = (lane // 4) <= rem
    is_key = (lane % 4) < 2
    masks = []
    for head in range(2):
        mine = is_key & ((lane % 2) == head)
        masks.append((jnp.where(mine, 1.0, 0.0), jnp.where(mine & seen, 1.0, 0.0)))
    for p in range(pages):
        full = jnp.broadcast_to(whole[:, p : p + 1], (reqs, page_rows))
        part = jnp.broadcast_to(partial[:, p : p + 1], (reqs, page_rows))
        for head in range(2):
            weight[p, head] = full * masks[head][0] + part * masks[head][1]

    query = q_ref[...].astype(F32)
    heads = query.shape[1] // head_dim
    group = heads // 2
    stacked = jnp.concatenate(
        [query[:, h * head_dim : (h + 1) * head_dim] for h in range(heads)], axis=0
    ).astype(BF16)
    scale = math.log2(math.e) / math.sqrt(head_dim)
    step_rows = 2 * page_rows
    groups = 13
    steps = pages // (2 * groups)

    def rows_of(g, i):
        first = pl.multiple_of((g * steps + i) * step_rows, step_rows)
        return kv[pl.ds(first, step_rows), :]

    def score_group(g, top):
        tops = [top[h * reqs : (h + 1) * reqs, :] for h in range(heads)]
        for i in range(steps):
            s = dot_nt(stacked, rows_of(g, i))
            for half in range(2):
                p = (g * steps + i) * 2 + half
                bias = [jnp.where(weight[p, head] > 0, 0.0, -1e30) for head in range(2)]
                for h in range(heads):
                    piece = s[h * reqs : (h + 1) * reqs, half * page_rows : (half + 1) * page_rows]
                    masked = piece + bias[h // group]
                    scores[p, h * reqs : (h + 1) * reqs, :] = masked
                    tops[h] = jnp.maximum(tops[h], masked)
        return jnp.concatenate(tops, axis=0)

    def value_group(g, carry):
        total, acc = carry
        for i in range(steps):
            parts = []
            for half in range(2):
                p = (g * steps + i) * 2 + half
                w = jnp.concatenate([weight[p, h // group] for h in range(heads)], axis=0)
                e = jnp.exp2((scores[p] - top) * scale) * w
                total += e
                parts.append(pltpu.roll(e, 2, 1).astype(BF16))
            acc += dot_nn(jnp.concatenate(parts, axis=1), rows_of(g, i))
        return total, acc

    for copy in loads:
        copy.wait()
    top = jnp.full((heads * reqs, page_rows), -1e30, F32)
    for g in range(groups):
        top = score_group(g, top)
    top = jnp.max(top, axis=1, keepdims=True)
    carry = (
        jnp.zeros((heads * reqs, page_rows), F32),
        jnp.zeros((heads * reqs, head_dim), F32),
    )
    for g in range(groups):
        carry = value_group(g, carry)
    total, acc = carry
    result = acc / jnp.sum(total, axis=1, keepdims=True)
    return jnp.concatenate(
        [result[h * reqs : (h + 1) * reqs, :] for h in range(heads)], axis=1
    ).astype(BF16)


Z_ORDER = (4, 3, 5, 2, 6, 1, 7)
PLANE_ORDER = (10, 8, 11, 9, 6, 14, 4, 12, 7, 15, 5, 13, 2, 3, 1)


def expert_kernel(
    page_len,
    lens_hbm,
    table_hbm,
    q_hbm,
    hidden_hbm,
    gain_hbm,
    router_hbm,
    ids_hbm,
    pool_hbm,
    ow_hbm,
    gu_hbm,
    down_hbm,
    out_ref,
    stat_ref,
    lens_s,
    table_v,
    q_ref,
    hidden_ref,
    gain_ref,
    ids_ref,
    kv,
    ow,
    scores,
    weight,
    part_ref,
    gu,
    down,
    pbuf,
    router2,
    zbuf,
    zbuf2,
    psend,
    xbuf,
    gu2,
    down2,
    rsend,
    rbuf,
    csend,
    fbuf,
    w_sem,
    kv_sem,
    z_send,
    z_recv,
    p_send,
    p_recv,
    y_sem,
    r_send,
    r_recv,
    c_send,
    c_recv,
    in_sem,
    ow_sem,
    small_sem,
):
    me = lax.axis_index("req")
    k = lax.axis_index("kv")
    core = lax.rem(me, 2)
    xh = lax.rem(lax.div(me, 2), 2)
    y = lax.rem(lax.div(me, 4), 4)
    z = lax.div(me, 16)
    line = y * 2 + xh
    sibling = me + 1 - 2 * core
    rows_y = [y] + [lax.rem(y + d, 4) for d in range(1, 4)]
    rows_x = [xh, 1 - xh]
    rows_k = [k, 1 - k]
    rows_z = [z] + [lax.rem(z + d, 8) for d in range(1, 8)]
    corner = me - line * 2
    offset = me - z * 16

    def plane_peer(i):
        block = rows_y[i // 4] * 2 + rows_x[(i // 2) % 2]
        return corner + block * 2, rows_k[i % 2], block

    def z_peer(d):
        return rows_z[d] * 16 + offset

    experts = router_hbm.shape[0]
    small = [
        pltpu.make_async_copy(source, target, small_sem.at[i])
        for i, (source, target) in enumerate(
            (
                (lens_hbm, lens_s),
                (table_hbm, table_v),
                (q_hbm, q_ref),
                (ids_hbm, ids_ref),
                (hidden_hbm, hidden_ref),
                (gain_hbm, gain_ref),
                (router_hbm, router2.at[pl.ds(0, experts)]),
                (router_hbm, router2.at[pl.ds(experts, experts)]),
            )
        )
    ]
    for copy in small[:3]:
        copy.start()
    chunks = in_sem.shape[0]
    chunk = kv.shape[0] // chunks
    loads = [
        pltpu.make_async_copy(
            pool_hbm.at[pl.ds(i * chunk, chunk)], kv.at[pl.ds(i * chunk, chunk)], in_sem.at[i]
        )
        for i in range(chunks)
    ]
    ow_chunks = ow_sem.shape[0]
    ow_chunk = ow.shape[0] // ow_chunks
    ow_loads = [
        pltpu.make_async_copy(
            ow_hbm.at[pl.ds(i * ow_chunk, ow_chunk)],
            ow.at[pl.ds(i * ow_chunk, ow_chunk)],
            ow_sem.at[i],
        )
        for i in range(ow_chunks)
    ]
    w_loads = [
        pltpu.make_async_copy(gu_hbm.at[0], gu.at[0], w_sem.at[0]),
        pltpu.make_async_copy(gu_hbm.at[1], gu.at[1], w_sem.at[1]),
        pltpu.make_async_copy(down_hbm, down, w_sem.at[2]),
    ]
    for copy in loads + ow_loads + small[3:]:
        copy.start()
    barrier = pltpu.get_barrier_semaphore()
    for i in range(1, 16):
        dev, pk, _ = plane_peer(i)
        pl.semaphore_signal(barrier, inc=1, device_id=(dev, pk), device_id_type=MESH)
    for d in range(1, 8):
        for side in range(2):
            pl.semaphore_signal(barrier, inc=1, device_id=(z_peer(d), side), device_id_type=MESH)
    pl.semaphore_signal(barrier, inc=1, device_id=(sibling, k), device_id_type=MESH)

    for copy in small[:3]:
        copy.wait()
    attended = attend(page_len, table_v, lens_s, q_ref, kv, scores, weight, loads)
    for copy in small[3:]:
        copy.wait()
    for copy in ow_loads:
        copy.wait()
    for copy in w_loads:
        copy.start()
    part_ref[...] = dot_nn(attended, ow[...]).astype(BF16)
    pl.semaphore_wait(barrier, 30)

    swap = pltpu.make_async_remote_copy(
        src_ref=part_ref,
        dst_ref=pbuf,
        send_sem=kv_sem.at[0],
        recv_sem=kv_sem.at[1],
        device_id=(me, 1 - k),
        device_id_type=MESH,
    )
    swap.start()
    lends = []
    for i, (source, target) in enumerate(
        ((gu_hbm.at[0], gu2.at[0]), (gu_hbm.at[1], gu2.at[1]), (down_hbm, down2))
    ):
        copy = pltpu.make_async_remote_copy(
            src_ref=source,
            dst_ref=target,
            send_sem=y_sem.at[2 * i],
            recv_sem=y_sem.at[2 * i + 1],
            device_id=(sibling, k),
            device_id_type=MESH,
        )
        copy.start()
        lends.append(copy)
    tokens, width = hidden_ref.shape
    half = width // 2
    chosen_count = ids_ref.shape[1]
    lane = lax.broadcasted_iota(jnp.int32, (tokens, 2 * experts), 1)
    chosen = jnp.zeros((tokens, 2 * experts), F32)
    for j in range(chosen_count):
        chosen += jnp.where(lane % experts == ids_ref[:, j : j + 1], 1.0, 0.0)
    swap.wait()
    projected = part_ref[...].astype(F32) + pbuf[...].astype(F32)
    mixed = (hidden_ref[...].astype(F32) + projected).astype(BF16).astype(F32)
    norms = jnp.sqrt(jnp.sum(mixed * mixed, axis=1, keepdims=True) / width + 1e-06)
    normed = (mixed / norms * gain_ref[...].astype(F32).reshape(1, width)).astype(BF16)
    logits = dot_nt(normed, router2[...])
    stat_ref[...] = jnp.where(
        lane == 0, norms, jnp.max(logits, axis=1, keepdims=True)
    )
    raised = jnp.where(chosen > 0, jnp.exp(logits), 0.0)
    gates = raised / jnp.sum(jnp.where(lane < experts, raised, 0.0), axis=1, keepdims=True)
    high = gates.astype(BF16).astype(F32)
    meta = jnp.where(lane < experts, jnp.where(chosen > 0, high, -1.0), gates - high)

    normed32 = normed.astype(F32)
    own_half = jnp.where(k == 0, normed32[:, :half], normed32[:, half:])
    part_width = half // 2
    zbuf[z] = jnp.concatenate([own_half[:, :part_width], meta], axis=1).astype(BF16)
    zbuf2[z] = own_half[:, part_width:].astype(BF16)
    z_copies = []
    for q, buffer in enumerate((zbuf, zbuf2)):
        for d in Z_ORDER:
            copy = pltpu.make_async_remote_copy(
                src_ref=buffer.at[z],
                dst_ref=buffer.at[z],
                send_sem=z_send.at[8 * q + d],
                recv_sem=z_recv.at[8 * q + d],
                device_id=(z_peer(d), k),
                device_id_type=MESH,
            )
            copy.start()
            z_copies.append(copy)

    count = 8 * tokens
    slots = 128
    row = lax.broadcasted_iota(jnp.int32, (slots, 2 * experts), 0)
    col = lax.broadcasted_iota(jnp.int32, (slots, 2 * experts), 1)
    pick_high = jnp.where(col == 8 * z + row // 16, 1.0, 0.0).astype(BF16)
    pick_low = jnp.where(col == experts + 8 * z + row // 16, 1.0, 0.0).astype(BF16)
    row = lax.broadcasted_iota(jnp.int32, (count, count), 0)
    col = lax.broadcasted_iota(jnp.int32, (count, count), 1)
    same = row // tokens == col // tokens
    before = jnp.where(same & (row < col), 1.0, 0.0).astype(BF16)
    after = jnp.where(same & (col < row), 1.0, 0.0).astype(BF16)

    for copy in z_copies[:7]:
        copy.wait_recv()
    gathered = zbuf[...].astype(F32).reshape(count, part_width + 2 * experts)
    metas = gathered[:, part_width:].astype(BF16)
    row = lax.broadcasted_iota(jnp.int32, (slots, count), 0)
    col = lax.broadcasted_iota(jnp.int32, (slots, count), 1)
    taken = jnp.where(dot_nt(pick_high, metas) >= 0, 1.0, 0.0)
    rank = dot_nn(taken.astype(BF16), before)
    hit = (taken > 0) & (col // tokens == (row // 2) % 8) & (rank == (row % 2).astype(F32))
    dispatch = jnp.where(hit, 1.0, 0.0).astype(BF16)
    p_copies = {}
    for q in range(2):
        if q == 0:
            states = gathered[:, :part_width].astype(BF16)
        else:
            for copy in z_copies[7:]:
                copy.wait_recv()
            states = zbuf2[...].astype(F32).reshape(count, part_width).astype(BF16)
        psend[q] = dot_nn(dispatch, states).reshape(8, 16, part_width).astype(BF16)
        for i in PLANE_ORDER:
            dev, pk, block = plane_peer(i)
            copy = pltpu.make_async_remote_copy(
                src_ref=psend.at[q, block],
                dst_ref=xbuf.at[k, q, line],
                send_sem=p_send.at[16 * q + i],
                recv_sem=p_recv.at[16 * q + i],
                device_id=(dev, pk),
                device_id_type=MESH,
            )
            copy.start()
            p_copies[16 * q + i] = copy
        xbuf[k, q, line] = psend[q, line]

    row = lax.broadcasted_iota(jnp.int32, (count, slots), 0)
    col = lax.broadcasted_iota(jnp.int32, (count, slots), 1)
    gate_high = dot_nt(metas, pick_high)
    gate_low = dot_nt(metas, pick_low)
    taken = jnp.where(gate_high >= 0, 1.0, 0.0)
    rank = dot_nn(after, taken.astype(BF16))
    hit = (taken > 0) & (row // tokens == (col // 2) % 8) & (rank == (col % 2).astype(F32))
    combine_high = jnp.where(hit, gate_high, 0.0).astype(BF16)
    combine_low = jnp.where(hit, gate_low, 0.0).astype(BF16)

    for copy in w_loads:
        copy.wait()
    for copy in lends:
        copy.wait_recv()
    sums = [jnp.zeros((slots, down.shape[0]), F32) for _ in range(4)]
    for q in range(2):
        for i in PLANE_ORDER:
            p_copies[16 * q + i].wait_recv()
        for part in range(2):
            block = xbuf[part, q].astype(F32).reshape(slots, part_width).astype(BF16)
            first = part * half + q * part_width
            for j, weights in enumerate((gu, gu2)):
                for side in range(2):
                    sums[2 * j + side] += dot_nt(
                        block, weights[side, :, first : first + part_width]
                    )
    acts = []
    for j in range(2):
        gate, up = sums[2 * j], sums[2 * j + 1]
        acts.append((gate / (1.0 + jnp.exp(-gate)) * up).astype(BF16))
    r_copies = []
    for q in range(2):
        for part in range(2):
            first = part * half + q * part_width
            last = first + part_width
            both = dot_nn(acts[0], down[:, first:last]) + dot_nn(acts[1], down2[:, first:last])
            rsend[q, part] = both.reshape(8, 16, part_width).astype(BF16)
        for i in PLANE_ORDER:
            dev, pk, block = plane_peer(i)
            copy = pltpu.make_async_remote_copy(
                src_ref=rsend.at[q, pk, block],
                dst_ref=rbuf.at[q, k, line],
                send_sem=r_send.at[16 * q + i],
                recv_sem=r_recv.at[16 * q + i],
                device_id=(dev, pk),
                device_id_type=MESH,
            )
            copy.start()
            r_copies.append(copy)
        rbuf[q, k, line] = rsend[q, k, line]
    c_copies = []
    for q in range(2):
        for copy in r_copies[15 * q : 15 * q + 15]:
            copy.wait_recv()
        routed = jnp.zeros((count, part_width), F32)
        for side in range(2):
            block = rbuf[q, side].astype(F32).reshape(slots, part_width).astype(BF16)
            routed += dot_nn(combine_high, block) + dot_nn(combine_low, block)
        csend[q] = routed.reshape(8, tokens, part_width).astype(BF16)
        for j, d in enumerate(Z_ORDER + (0,)):
            for flip in (1, 0):
                if d + flip > 0:
                    copy = pltpu.make_async_remote_copy(
                        src_ref=csend.at[q, rows_z[d]],
                        dst_ref=fbuf.at[q, k, z],
                        send_sem=c_send.at[16 * q + 2 * j + flip],
                        recv_sem=c_recv.at[16 * q + 2 * j + flip],
                        device_id=(z_peer(d), rows_k[flip]),
                        device_id_type=MESH,
                    )
                    copy.start()
                    c_copies.append(copy)
        fbuf[q, k, z] = csend[q, z]
    for q in range(2):
        for copy in c_copies[15 * q : 15 * q + 15]:
            copy.wait_recv()
        for side in range(2):
            total = jnp.sum(fbuf[q, side].astype(F32), axis=0)
            first = side * half + q * part_width
            last = first + part_width
            out_ref[:, first:last] = (mixed[:, first:last] + total).astype(BF16)
    for copy in lends + z_copies + list(p_copies.values()) + r_copies + c_copies:
        copy.wait_send()


def finish_kernel(hidden_ref, stat_ref, out_ref, norm_ref, logit_ref):
    out_ref[...] = hidden_ref[...]
    stats = stat_ref[...]
    row = lax.broadcasted_iota(jnp.int32, stats.shape, 0)
    col = lax.broadcasted_iota(jnp.int32, stats.shape, 1)
    for target, lane in ((norm_ref, 0), (logit_ref, 1)):
        column = jnp.broadcast_to(stats[:, lane : lane + 1], stats.shape)
        line = jnp.sum(jnp.where(row == col, column, 0.0), axis=0)
        target[...] = line[: target.shape[0]]


def to_rows(array):
    lead = math.prod(array.shape[:-2])
    head_dim = array.shape[-1] // 2
    split = array.reshape(lead, array.shape[-2], 2, head_dim)
    return split.transpose(0, 2, 1, 3).reshape(-1, head_dim)


def body(
    hidden,
    queries,
    fresh_key_value,
    kv_pool,
    page_table,
    lengths,
    out_weight,
    norm_gain,
    router_weight,
    expert_ids,
    expert_gate_up,
    expert_down,
):
    tokens, width = hidden.shape
    half = width // 2
    pages, page_len, kv_heads, pair = kv_pool.shape
    head_dim = pair // 2
    pool_rows = to_rows(kv_pool)
    fresh_rows = to_rows(fresh_key_value)
    rows = pool_rows.shape[0]
    heads = queries.shape[1] // head_dim
    page_rows = rows // pages
    vmem = pl.BlockSpec(memory_space=pltpu.VMEM)
    hbm = pl.BlockSpec(memory_space=pltpu.HBM)
    pool_new = pl.pallas_call(
        functools.partial(pool_kernel, page_len),
        out_shape=jax.ShapeDtypeStruct(pool_rows.shape, BF16),
        in_specs=[hbm, hbm, hbm, hbm],
        out_specs=hbm,
        scratch_shapes=[
            pltpu.SMEM(page_table.shape, jnp.int32),
            pltpu.SMEM(lengths.shape, jnp.int32),
            pltpu.VMEM(fresh_rows.shape, BF16),
            pltpu.VMEM(pool_rows.shape, BF16),
            pltpu.SemaphoreType.DMA((8,)),
            pltpu.SemaphoreType.DMA((8,)),
            pltpu.SemaphoreType.DMA((3,)),
        ],
    )(page_table, lengths, fresh_rows, pool_rows)
    updated_pool = (
        pool_new.reshape(pages * page_len, 2, kv_heads, head_dim)
        .transpose(0, 2, 1, 3)
        .reshape(kv_pool.shape)
    )
    gate_up = expert_gate_up[0]
    down = expert_down[0]
    experts = router_weight.shape[0]
    dma = pltpu.SemaphoreType.DMA
    out_raw, stats = pl.pallas_call(
        functools.partial(expert_kernel, page_len),
        out_shape=(
            jax.ShapeDtypeStruct((tokens, width), BF16),
            jax.ShapeDtypeStruct((tokens, 2 * experts), F32),
        ),
        in_specs=[hbm] * 11,
        out_specs=(vmem, vmem),
        scratch_shapes=[
            pltpu.SMEM(lengths.shape, jnp.int32),
            pltpu.VMEM(page_table.shape, jnp.int32),
            pltpu.VMEM(queries.shape, BF16),
            pltpu.VMEM(hidden.shape, BF16),
            pltpu.VMEM(norm_gain.shape, BF16),
            pltpu.VMEM(expert_ids.shape, jnp.int32),
            pltpu.VMEM(pool_rows.shape, BF16),
            pltpu.VMEM(out_weight.shape, BF16),
            pltpu.VMEM((pages, heads * tokens, page_rows), F32),
            pltpu.VMEM((pages, 2, tokens, page_rows), F32),
            pltpu.VMEM((tokens, width), BF16),
            pltpu.VMEM(gate_up.shape, BF16),
            pltpu.VMEM(down.shape, BF16),
            pltpu.VMEM((tokens, width), BF16),
            pltpu.VMEM((2 * experts, width), BF16),
            pltpu.VMEM((8, tokens, half // 2 + 2 * experts), BF16),
            pltpu.VMEM((8, tokens, half // 2), BF16),
            pltpu.VMEM((2, 8, 16, half // 2), BF16),
            pltpu.VMEM((2, 2, 8, 16, half // 2), BF16),
            pltpu.VMEM(gate_up.shape, BF16),
            pltpu.VMEM(down.shape, BF16),
            pltpu.VMEM((2, 2, 8, 16, half // 2), BF16),
            pltpu.VMEM((2, 2, 8, 16, half // 2), BF16),
            pltpu.VMEM((2, 8, tokens, half // 2), BF16),
            pltpu.VMEM((2, 2, 8, tokens, half // 2), BF16),
            dma((3,)),
            dma((2,)),
            dma((16,)),
            dma((16,)),
            dma((32,)),
            dma((32,)),
            dma((6,)),
            dma((32,)),
            dma((32,)),
            dma((32,)),
            dma((32,)),
            dma((13,)),
            dma((4,)),
            dma((8,)),
        ],
        compiler_params=pltpu.CompilerParams(collective_id=0, has_side_effects=True),
    )(
        lengths,
        page_table,
        queries,
        hidden,
        norm_gain,
        router_weight,
        expert_ids,
        pool_new,
        out_weight,
        gate_up,
        down,
    )
    out_hidden, norms, max_logit = pl.pallas_call(
        finish_kernel,
        out_shape=(
            jax.ShapeDtypeStruct((tokens, width), BF16),
            jax.ShapeDtypeStruct((tokens,), F32),
            jax.ShapeDtypeStruct((tokens,), F32),
        ),
        in_specs=[vmem, vmem],
        out_specs=(vmem, vmem, vmem),
    )(out_raw, stats)
    return (out_hidden, updated_pool, norms, max_logit)


def solution(mesh):
    in_specs = (
        P("req", None),
        P("req", "kv"),
        P("req", "kv", None),
        P("req", None, "kv", None),
        P("req", None),
        P("req"),
        P("kv", None),
        P(),
        P(),
        P("req", None),
        P("req", None, "kv", None),
        P("req", "kv", None),
    )
    out_specs = (P("req", None), P("req", None, "kv", None), P("req"), P("req"))
    return jax.shard_map(body, mesh=mesh, in_specs=in_specs, out_specs=out_specs, check_vma=False)
```

```python
import functools
import math

import jax
import jax.numpy as jnp
from jax import lax
from jax.experimental import pallas as pl
from jax.experimental.pallas import tpu as pltpu
from jax.sharding import PartitionSpec as P

MESH = pl.DeviceIdType.MESH
F32 = jnp.float32
BF16 = jnp.bfloat16


def dot_nn(a, b):
    return lax.dot_general(a, b, (((1,), (0,)), ((), ())), preferred_element_type=F32)


def dot_nt(a, b):
    return lax.dot_general(a, b, (((1,), (1,)), ((), ())), preferred_element_type=F32)


def pool_kernel(
    page_len,
    table_hbm,
    lens_hbm,
    fresh_hbm,
    pool_hbm,
    pool_out,
    table_s,
    lens_s,
    fresh_ref,
    kv,
    in_sem,
    out_sem,
    small_sem,
):
    reqs = table_s.shape[0]
    head_dim = kv.shape[1]
    chunks = in_sem.shape[0]
    chunk = kv.shape[0] // chunks
    loads = [
        pltpu.make_async_copy(
            pool_hbm.at[pl.ds(i * chunk, chunk)], kv.at[pl.ds(i * chunk, chunk)], in_sem.at[i]
        )
        for i in range(chunks)
    ]
    small = [
        pltpu.make_async_copy(source, target, small_sem.at[i])
        for i, (source, target) in enumerate(
            ((table_hbm, table_s), (lens_hbm, lens_s), (fresh_hbm, fresh_ref))
        )
    ]
    for copy in small + loads:
        copy.start()
    row = lax.broadcasted_iota(jnp.int32, (16, head_dim), 0)
    bases, news = [], []
    for copy in small:
        copy.wait()
    for r in range(reqs):
        length = lens_s[r]
        page = table_s[r, length // page_len]
        position = page * page_len + length % page_len
        bases.append(position // 4)
        four = fresh_ref[4 * r : 4 * r + 4, :].astype(F32)
        news.append((row // 4 == position % 4, jnp.concatenate([four, four, four, four], axis=0)))
    stores = []
    for i in range(chunks):
        loads[i].wait()
        for r in range(reqs):

            @pl.when(bases[r] // (chunk // 16) == i)
            def _():
                base = pl.multiple_of(bases[r] * 16, 16)
                hit, tiled = news[r]
                old = kv[pl.ds(base, 16), :].astype(F32)
                kv[pl.ds(base, 16), :] = jnp.where(hit, tiled, old).astype(BF16)

        copy = pltpu.make_async_copy(
            kv.at[pl.ds(i * chunk, chunk)], pool_out.at[pl.ds(i * chunk, chunk)], out_sem.at[i]
        )
        copy.start()
        stores.append(copy)
    for copy in stores:
        copy.wait()


def attend(page_len, table_v, lens_s, q_ref, kv, scores, weight, loads):
    reqs, max_pages = table_v.shape
    head_dim = kv.shape[1]
    page_rows = 4 * page_len
    pages = kv.shape[0] // page_rows
    req_row = lax.broadcasted_iota(jnp.int32, (reqs, page_rows), 0)
    lane = lax.broadcasted_iota(jnp.int32, (reqs, page_rows), 1)
    lens = jnp.zeros((reqs, page_rows), jnp.int32)
    for r in range(reqs):
        lens = jnp.where(req_row == r, lens_s[r], lens)
    last_page = lens // page_len
    rem = lens % page_len
    whole = jnp.zeros((reqs, page_rows), F32)
    partial = jnp.zeros((reqs, page_rows), F32)
    for j in range(max_pages):
        named = lane == table_v[:, j : j + 1]
        whole += jnp.where(named & (last_page > j), 1.0, 0.0)
        partial += jnp.where(named & (last_page == j), 1.0, 0.0)
    seen = (lane // 4) <= rem
    is_key = (lane % 4) < 2
    masks = []
    for head in range(2):
        mine = is_key & ((lane % 2) == head)
        masks.append((jnp.where(mine, 1.0, 0.0), jnp.where(mine & seen, 1.0, 0.0)))
    for p in range(pages):
        full = jnp.broadcast_to(whole[:, p : p + 1], (reqs, page_rows))
        part = jnp.broadcast_to(partial[:, p : p + 1], (reqs, page_rows))
        for head in range(2):
            weight[p, head] = full * masks[head][0] + part * masks[head][1]

    query = q_ref[...].astype(F32)
    heads = query.shape[1] // head_dim
    group = heads // 2
    stacked = jnp.concatenate(
        [query[:, h * head_dim : (h + 1) * head_dim] for h in range(heads)], axis=0
    ).astype(BF16)
    scale = math.log2(math.e) / math.sqrt(head_dim)
    step_rows = 2 * page_rows
    groups = 13
    steps = pages // (2 * groups)

    def rows_of(g, i):
        first = pl.multiple_of((g * steps + i) * step_rows, step_rows)
        return kv[pl.ds(first, step_rows), :]

    def score_group(g, top):
        tops = [top[h * reqs : (h + 1) * reqs, :] for h in range(heads)]
        for i in range(steps):
            s = dot_nt(stacked, rows_of(g, i))
            for half in range(2):
                p = (g * steps + i) * 2 + half
                bias = [jnp.where(weight[p, head] > 0, 0.0, -1e30) for head in range(2)]
                for h in range(heads):
                    piece = s[h * reqs : (h + 1) * reqs, half * page_rows : (half + 1) * page_rows]
                    masked = piece + bias[h // group]
                    scores[p, h * reqs : (h + 1) * reqs, :] = masked
                    tops[h] = jnp.maximum(tops[h], masked)
        return jnp.concatenate(tops, axis=0)

    def value_group(g, carry):
        total, acc = carry
        for i in range(steps):
            parts = []
            for half in range(2):
                p = (g * steps + i) * 2 + half
                w = jnp.concatenate([weight[p, h // group] for h in range(heads)], axis=0)
                e = jnp.exp2((scores[p] - top) * scale) * w
                total += e
                parts.append(pltpu.roll(e, 2, 1).astype(BF16))
            acc += dot_nn(jnp.concatenate(parts, axis=1), rows_of(g, i))
        return total, acc

    for copy in loads:
        copy.wait()
    top = jnp.full((heads * reqs, page_rows), -1e30, F32)
    for g in range(groups):
        top = score_group(g, top)
    top = jnp.max(top, axis=1, keepdims=True)
    carry = (
        jnp.zeros((heads * reqs, page_rows), F32),
        jnp.zeros((heads * reqs, head_dim), F32),
    )
    for g in range(groups):
        carry = value_group(g, carry)
    total, acc = carry
    result = acc / jnp.sum(total, axis=1, keepdims=True)
    return jnp.concatenate(
        [result[h * reqs : (h + 1) * reqs, :] for h in range(heads)], axis=1
    ).astype(BF16)


Z_ORDER = (4, 3, 5, 2, 6, 1, 7)
PLANE_ORDER = (10, 8, 11, 9, 6, 14, 4, 12, 7, 15, 5, 13, 2, 3, 1)


def expert_kernel(
    page_len,
    lens_hbm,
    table_hbm,
    q_hbm,
    hidden_hbm,
    gain_hbm,
    router_hbm,
    ids_hbm,
    pool_hbm,
    ow_hbm,
    gu_hbm,
    down_hbm,
    out_ref,
    stat_ref,
    lens_s,
    table_v,
    q_ref,
    hidden_ref,
    gain_ref,
    ids_ref,
    kv,
    ow,
    scores,
    weight,
    part_ref,
    gu,
    down,
    pbuf,
    router2,
    ibuf,
    gbuf,
    zbuf,
    zbuf2,
    psend,
    xbuf,
    gu2,
    down2,
    rsend,
    rbuf,
    csend,
    fbuf,
    w_sem,
    kv_sem,
    z_send,
    z_recv,
    p_send,
    p_recv,
    y_sem,
    r_send,
    r_recv,
    c_send,
    c_recv,
    in_sem,
    ow_sem,
    small_sem,
):
    me = lax.axis_index("req")
    k = lax.axis_index("kv")
    core = lax.rem(me, 2)
    xh = lax.rem(lax.div(me, 2), 2)
    y = lax.rem(lax.div(me, 4), 4)
    z = lax.div(me, 16)
    line = y * 2 + xh
    sibling = me + 1 - 2 * core
    rows_y = [y] + [lax.rem(y + d, 4) for d in range(1, 4)]
    rows_x = [xh, 1 - xh]
    rows_k = [k, 1 - k]
    rows_z = [z] + [lax.rem(z + d, 8) for d in range(1, 8)]
    corner = me - line * 2
    offset = me - z * 16

    def plane_peer(i):
        block = rows_y[i // 4] * 2 + rows_x[(i // 2) % 2]
        return corner + block * 2, rows_k[i % 2], block

    def z_peer(d):
        return rows_z[d] * 16 + offset

    experts = router_hbm.shape[0]
    small = [
        pltpu.make_async_copy(source, target, small_sem.at[i])
        for i, (source, target) in enumerate(
            (
                (lens_hbm, lens_s),
                (table_hbm, table_v),
                (q_hbm, q_ref),
                (ids_hbm, ids_ref),
                (hidden_hbm, hidden_ref),
                (gain_hbm, gain_ref),
                (router_hbm, router2.at[pl.ds(0, experts)]),
                (router_hbm, router2.at[pl.ds(experts, experts)]),
            )
        )
    ]
    for copy in small[:3]:
        copy.start()
    chunks = in_sem.shape[0]
    chunk = kv.shape[0] // chunks
    loads = [
        pltpu.make_async_copy(
            pool_hbm.at[pl.ds(i * chunk, chunk)], kv.at[pl.ds(i * chunk, chunk)], in_sem.at[i]
        )
        for i in range(chunks)
    ]
    ow_chunks = ow_sem.shape[0]
    ow_chunk = ow.shape[0] // ow_chunks
    ow_loads = [
        pltpu.make_async_copy(
            ow_hbm.at[pl.ds(i * ow_chunk, ow_chunk)],
            ow.at[pl.ds(i * ow_chunk, ow_chunk)],
            ow_sem.at[i],
        )
        for i in range(ow_chunks)
    ]
    w_loads = [
        pltpu.make_async_copy(gu_hbm.at[0], gu.at[0], w_sem.at[0]),
        pltpu.make_async_copy(gu_hbm.at[1], gu.at[1], w_sem.at[1]),
        pltpu.make_async_copy(down_hbm, down, w_sem.at[2]),
    ]
    for copy in loads + ow_loads + small[3:]:
        copy.start()
    barrier = pltpu.get_barrier_semaphore()
    for i in range(1, 16):
        dev, pk, _ = plane_peer(i)
        pl.semaphore_signal(barrier, inc=1, device_id=(dev, pk), device_id_type=MESH)
    for d in range(1, 8):
        for side in range(2):
            pl.semaphore_signal(barrier, inc=1, device_id=(z_peer(d), side), device_id_type=MESH)
    pl.semaphore_signal(barrier, inc=1, device_id=(sibling, k), device_id_type=MESH)

    for copy in small[:3]:
        copy.wait()
    attended = attend(page_len, table_v, lens_s, q_ref, kv, scores, weight, loads)
    for copy in small[3:]:
        copy.wait()
    for copy in ow_loads:
        copy.wait()
    for copy in w_loads:
        copy.start()
    part_ref[...] = dot_nn(attended, ow[...]).astype(BF16)
    tokens, width = hidden_ref.shape
    half = width // 2
    chosen_count = ids_ref.shape[1]
    lane = lax.broadcasted_iota(jnp.int32, (tokens, 2 * experts), 1)
    chosen = jnp.zeros((tokens, 2 * experts), F32)
    for j in range(chosen_count):
        chosen += jnp.where(lane % experts == ids_ref[:, j : j + 1], 1.0, 0.0)
    ibuf[z] = chosen.astype(BF16)
    pl.semaphore_wait(barrier, 30)

    swap = pltpu.make_async_remote_copy(
        src_ref=part_ref,
        dst_ref=pbuf,
        send_sem=kv_sem.at[0],
        recv_sem=kv_sem.at[1],
        device_id=(me, 1 - k),
        device_id_type=MESH,
    )
    swap.start()
    lends = []
    for i, (source, target) in enumerate(
        ((gu_hbm.at[0], gu2.at[0]), (gu_hbm.at[1], gu2.at[1]), (down_hbm, down2))
    ):
        copy = pltpu.make_async_remote_copy(
            src_ref=source,
            dst_ref=target,
            send_sem=y_sem.at[2 * i],
            recv_sem=y_sem.at[2 * i + 1],
            device_id=(sibling, k),
            device_id_type=MESH,
        )
        copy.start()
        lends.append(copy)

    def along_z(buffer, send, recv, first):
        copies = []
        for d in Z_ORDER:
            copy = pltpu.make_async_remote_copy(
                src_ref=buffer.at[z],
                dst_ref=buffer.at[z],
                send_sem=send.at[first + d],
                recv_sem=recv.at[first + d],
                device_id=(z_peer(d), k),
                device_id_type=MESH,
            )
            copy.start()
            copies.append(copy)
        return copies

    z_copies = along_z(ibuf, z_send, z_recv, 16)
    swap.wait()
    projected = part_ref[...].astype(F32) + pbuf[...].astype(F32)
    mixed = (hidden_ref[...].astype(F32) + projected).astype(BF16).astype(F32)
    norms = jnp.sqrt(jnp.sum(mixed * mixed, axis=1, keepdims=True) / width + 1e-06)
    normed = (mixed / norms * gain_ref[...].astype(F32).reshape(1, width)).astype(BF16)
    normed32 = normed.astype(F32)
    own_half = jnp.where(k == 0, normed32[:, :half], normed32[:, half:])
    part_width = half // 2
    for q, buffer in enumerate((zbuf, zbuf2)):
        buffer[z] = own_half[:, q * part_width : (q + 1) * part_width].astype(BF16)
        z_copies += along_z(buffer, z_send, z_recv, 8 * q)
    logits = dot_nt(normed, router2[...])
    stat_ref[...] = jnp.where(
        lane == 0, norms, jnp.max(logits, axis=1, keepdims=True)
    )
    raised = jnp.where(chosen > 0, jnp.exp(logits), 0.0)
    gates = raised / jnp.sum(jnp.where(lane < experts, raised, 0.0), axis=1, keepdims=True)
    high = gates.astype(BF16).astype(F32)
    meta = jnp.where(lane < experts, high, gates - high)

    gbuf[z] = meta.astype(BF16)
    z_copies += along_z(gbuf, z_send, z_recv, 24)

    count = 8 * tokens
    slots = 128
    row = lax.broadcasted_iota(jnp.int32, (slots, 2 * experts), 0)
    col = lax.broadcasted_iota(jnp.int32, (slots, 2 * experts), 1)
    pick_high = jnp.where(col == 8 * z + row // 16, 1.0, 0.0).astype(BF16)
    pick_low = jnp.where(col == experts + 8 * z + row // 16, 1.0, 0.0).astype(BF16)
    row = lax.broadcasted_iota(jnp.int32, (count, count), 0)
    col = lax.broadcasted_iota(jnp.int32, (count, count), 1)
    same = row // tokens == col // tokens
    before = jnp.where(same & (row < col), 1.0, 0.0).astype(BF16)
    after = jnp.where(same & (col < row), 1.0, 0.0).astype(BF16)

    for copy in z_copies[:7]:
        copy.wait_recv()
    flags = ibuf[...].astype(F32).reshape(count, 2 * experts).astype(BF16)
    row = lax.broadcasted_iota(jnp.int32, (slots, count), 0)
    col = lax.broadcasted_iota(jnp.int32, (slots, count), 1)
    taken = dot_nt(pick_high, flags)
    rank = dot_nn(taken.astype(BF16), before)
    hit = (taken > 0) & (col // tokens == (row // 2) % 8) & (rank == (row % 2).astype(F32))
    dispatch = jnp.where(hit, 1.0, 0.0).astype(BF16)
    p_copies = {}
    for q in range(2):
        for copy in z_copies[7 * q + 7 : 7 * q + 14]:
            copy.wait_recv()
        states = (zbuf, zbuf2)[q][...].astype(F32).reshape(count, part_width).astype(BF16)
        psend[q] = dot_nn(dispatch, states).reshape(8, 16, part_width).astype(BF16)
        for i in PLANE_ORDER:
            dev, pk, block = plane_peer(i)
            copy = pltpu.make_async_remote_copy(
                src_ref=psend.at[q, block],
                dst_ref=xbuf.at[k, q, line],
                send_sem=p_send.at[16 * q + i],
                recv_sem=p_recv.at[16 * q + i],
                device_id=(dev, pk),
                device_id_type=MESH,
            )
            copy.start()
            p_copies[16 * q + i] = copy
        xbuf[k, q, line] = psend[q, line]

    row = lax.broadcasted_iota(jnp.int32, (count, slots), 0)
    col = lax.broadcasted_iota(jnp.int32, (count, slots), 1)
    for copy in z_copies[21:]:
        copy.wait_recv()
    metas = gbuf[...].astype(F32).reshape(count, 2 * experts).astype(BF16)
    gate_high = dot_nt(metas, pick_high)
    gate_low = dot_nt(metas, pick_low)
    taken = dot_nt(flags, pick_high)
    rank = dot_nn(after, taken.astype(BF16))
    hit = (taken > 0) & (row // tokens == (col // 2) % 8) & (rank == (col % 2).astype(F32))
    combine_high = jnp.where(hit, gate_high, 0.0).astype(BF16)
    combine_low = jnp.where(hit, gate_low, 0.0).astype(BF16)

    for copy in w_loads:
        copy.wait()
    sums = [jnp.zeros((slots, down.shape[0]), F32) for _ in range(4)]
    for q in range(2):
        for i in PLANE_ORDER:
            p_copies[16 * q + i].wait_recv()
        blocks = [
            xbuf[part, q].astype(F32).reshape(slots, part_width).astype(BF16) for part in range(2)
        ]
        for j, weights in enumerate((gu, gu2)):
            if q == 0 and j == 1:
                for copy in lends[:2]:
                    copy.wait_recv()
            for part in range(2):
                first = part * half + q * part_width
                for side in range(2):
                    sums[2 * j + side] += dot_nt(
                        blocks[part], weights[side, :, first : first + part_width]
                    )
    lends[2].wait_recv()
    acts = []
    for j in range(2):
        gate, up = sums[2 * j], sums[2 * j + 1]
        acts.append((gate / (1.0 + jnp.exp(-gate)) * up).astype(BF16))
    r_copies = []
    for q in range(2):
        for part in range(2):
            first = part * half + q * part_width
            last = first + part_width
            both = dot_nn(acts[0], down[:, first:last]) + dot_nn(acts[1], down2[:, first:last])
            rsend[q, part] = both.reshape(8, 16, part_width).astype(BF16)
        for i in PLANE_ORDER:
            dev, pk, block = plane_peer(i)
            copy = pltpu.make_async_remote_copy(
                src_ref=rsend.at[q, pk, block],
                dst_ref=rbuf.at[q, k, line],
                send_sem=r_send.at[16 * q + i],
                recv_sem=r_recv.at[16 * q + i],
                device_id=(dev, pk),
                device_id_type=MESH,
            )
            copy.start()
            r_copies.append(copy)
        rbuf[q, k, line] = rsend[q, k, line]
    c_copies = []
    for q in range(2):
        for copy in r_copies[15 * q : 15 * q + 15]:
            copy.wait_recv()
        routed = jnp.zeros((count, part_width), F32)
        for side in range(2):
            block = rbuf[q, side].astype(F32).reshape(slots, part_width).astype(BF16)
            routed += dot_nn(combine_high, block) + dot_nn(combine_low, block)
        csend[q] = routed.reshape(8, tokens, part_width).astype(BF16)
        for j, d in enumerate(Z_ORDER + (0,)):
            for flip in (1, 0):
                if d + flip > 0:
                    copy = pltpu.make_async_remote_copy(
                        src_ref=csend.at[q, rows_z[d]],
                        dst_ref=fbuf.at[q, k, z],
                        send_sem=c_send.at[16 * q + 2 * j + flip],
                        recv_sem=c_recv.at[16 * q + 2 * j + flip],
                        device_id=(z_peer(d), rows_k[flip]),
                        device_id_type=MESH,
                    )
                    copy.start()
                    c_copies.append(copy)
        fbuf[q, k, z] = csend[q, z]
    for q in range(2):
        for copy in c_copies[15 * q : 15 * q + 15]:
            copy.wait_recv()
        for side in range(2):
            total = jnp.sum(fbuf[q, side].astype(F32), axis=0)
            first = side * half + q * part_width
            last = first + part_width
            out_ref[:, first:last] = (mixed[:, first:last] + total).astype(BF16)
    for copy in lends + z_copies + list(p_copies.values()) + r_copies + c_copies:
        copy.wait_send()


def finish_kernel(hidden_ref, stat_ref, out_ref, norm_ref, logit_ref):
    out_ref[...] = hidden_ref[...]
    stats = stat_ref[...]
    row = lax.broadcasted_iota(jnp.int32, stats.shape, 0)
    col = lax.broadcasted_iota(jnp.int32, stats.shape, 1)
    for target, lane in ((norm_ref, 0), (logit_ref, 1)):
        column = jnp.broadcast_to(stats[:, lane : lane + 1], stats.shape)
        line = jnp.sum(jnp.where(row == col, column, 0.0), axis=0)
        target[...] = line[: target.shape[0]]


def to_rows(array):
    lead = math.prod(array.shape[:-2])
    head_dim = array.shape[-1] // 2
    split = array.reshape(lead, array.shape[-2], 2, head_dim)
    return split.transpose(0, 2, 1, 3).reshape(-1, head_dim)


def body(
    hidden,
    queries,
    fresh_key_value,
    kv_pool,
    page_table,
    lengths,
    out_weight,
    norm_gain,
    router_weight,
    expert_ids,
    expert_gate_up,
    expert_down,
):
    tokens, width = hidden.shape
    half = width // 2
    pages, page_len, kv_heads, pair = kv_pool.shape
    head_dim = pair // 2
    pool_rows = to_rows(kv_pool)
    fresh_rows = to_rows(fresh_key_value)
    rows = pool_rows.shape[0]
    heads = queries.shape[1] // head_dim
    page_rows = rows // pages
    vmem = pl.BlockSpec(memory_space=pltpu.VMEM)
    hbm = pl.BlockSpec(memory_space=pltpu.HBM)
    pool_new = pl.pallas_call(
        functools.partial(pool_kernel, page_len),
        out_shape=jax.ShapeDtypeStruct(pool_rows.shape, BF16),
        in_specs=[hbm, hbm, hbm, hbm],
        out_specs=hbm,
        scratch_shapes=[
            pltpu.SMEM(page_table.shape, jnp.int32),
            pltpu.SMEM(lengths.shape, jnp.int32),
            pltpu.VMEM(fresh_rows.shape, BF16),
            pltpu.VMEM(pool_rows.shape, BF16),
            pltpu.SemaphoreType.DMA((8,)),
            pltpu.SemaphoreType.DMA((8,)),
            pltpu.SemaphoreType.DMA((3,)),
        ],
    )(page_table, lengths, fresh_rows, pool_rows)
    updated_pool = (
        pool_new.reshape(pages * page_len, 2, kv_heads, head_dim)
        .transpose(0, 2, 1, 3)
        .reshape(kv_pool.shape)
    )
    gate_up = expert_gate_up[0]
    down = expert_down[0]
    experts = router_weight.shape[0]
    dma = pltpu.SemaphoreType.DMA
    out_raw, stats = pl.pallas_call(
        functools.partial(expert_kernel, page_len),
        out_shape=(
            jax.ShapeDtypeStruct((tokens, width), BF16),
            jax.ShapeDtypeStruct((tokens, 2 * experts), F32),
        ),
        in_specs=[hbm] * 11,
        out_specs=(vmem, vmem),
        scratch_shapes=[
            pltpu.SMEM(lengths.shape, jnp.int32),
            pltpu.VMEM(page_table.shape, jnp.int32),
            pltpu.VMEM(queries.shape, BF16),
            pltpu.VMEM(hidden.shape, BF16),
            pltpu.VMEM(norm_gain.shape, BF16),
            pltpu.VMEM(expert_ids.shape, jnp.int32),
            pltpu.VMEM(pool_rows.shape, BF16),
            pltpu.VMEM(out_weight.shape, BF16),
            pltpu.VMEM((pages, heads * tokens, page_rows), F32),
            pltpu.VMEM((pages, 2, tokens, page_rows), F32),
            pltpu.VMEM((tokens, width), BF16),
            pltpu.VMEM(gate_up.shape, BF16),
            pltpu.VMEM(down.shape, BF16),
            pltpu.VMEM((tokens, width), BF16),
            pltpu.VMEM((2 * experts, width), BF16),
            pltpu.VMEM((8, tokens, 2 * experts), BF16),
            pltpu.VMEM((8, tokens, 2 * experts), BF16),
            pltpu.VMEM((8, tokens, half // 2), BF16),
            pltpu.VMEM((8, tokens, half // 2), BF16),
            pltpu.VMEM((2, 8, 16, half // 2), BF16),
            pltpu.VMEM((2, 2, 8, 16, half // 2), BF16),
            pltpu.VMEM(gate_up.shape, BF16),
            pltpu.VMEM(down.shape, BF16),
            pltpu.VMEM((2, 2, 8, 16, half // 2), BF16),
            pltpu.VMEM((2, 2, 8, 16, half // 2), BF16),
            pltpu.VMEM((2, 8, tokens, half // 2), BF16),
            pltpu.VMEM((2, 2, 8, tokens, half // 2), BF16),
            dma((3,)),
            dma((2,)),
            dma((32,)),
            dma((32,)),
            dma((32,)),
            dma((32,)),
            dma((6,)),
            dma((32,)),
            dma((32,)),
            dma((32,)),
            dma((32,)),
            dma((13,)),
            dma((4,)),
            dma((8,)),
        ],
        compiler_params=pltpu.CompilerParams(collective_id=0, has_side_effects=True),
    )(
        lengths,
        page_table,
        queries,
        hidden,
        norm_gain,
        router_weight,
        expert_ids,
        pool_new,
        out_weight,
        gate_up,
        down,
    )
    out_hidden, norms, max_logit = pl.pallas_call(
        finish_kernel,
        out_shape=(
            jax.ShapeDtypeStruct((tokens, width), BF16),
            jax.ShapeDtypeStruct((tokens,), F32),
            jax.ShapeDtypeStruct((tokens,), F32),
        ),
        in_specs=[vmem, vmem],
        out_specs=(vmem, vmem, vmem),
    )(out_raw, stats)
    return (out_hidden, updated_pool, norms, max_logit)


def solution(mesh):
    in_specs = (
        P("req", None),
        P("req", "kv"),
        P("req", "kv", None),
        P("req", None, "kv", None),
        P("req", None),
        P("req"),
        P("kv", None),
        P(),
        P(),
        P("req", None),
        P("req", None, "kv", None),
        P("req", "kv", None),
    )
    out_specs = (P("req", None), P("req", None, "kv", None), P("req"), P("req"))
    return jax.shard_map(body, mesh=mesh, in_specs=in_specs, out_specs=out_specs, check_vma=False)
```

```python
import functools
import math

import jax
import jax.numpy as jnp
from jax import lax
from jax.experimental import pallas as pl
from jax.experimental.pallas import tpu as pltpu
from jax.sharding import PartitionSpec as P

MESH = pl.DeviceIdType.MESH
F32 = jnp.float32
BF16 = jnp.bfloat16


def dot_nn(a, b):
    return lax.dot_general(a, b, (((1,), (0,)), ((), ())), preferred_element_type=F32)


def dot_nt(a, b):
    return lax.dot_general(a, b, (((1,), (1,)), ((), ())), preferred_element_type=F32)


def pool_kernel(
    page_len,
    table_hbm,
    lens_hbm,
    fresh_hbm,
    pool_hbm,
    pool_out,
    table_s,
    lens_s,
    fresh_ref,
    kv,
    in_sem,
    out_sem,
    small_sem,
):
    reqs = table_s.shape[0]
    head_dim = kv.shape[1]
    chunks = in_sem.shape[0]
    chunk = kv.shape[0] // chunks
    loads = [
        pltpu.make_async_copy(
            pool_hbm.at[pl.ds(i * chunk, chunk)], kv.at[pl.ds(i * chunk, chunk)], in_sem.at[i]
        )
        for i in range(chunks)
    ]
    small = [
        pltpu.make_async_copy(source, target, small_sem.at[i])
        for i, (source, target) in enumerate(
            ((table_hbm, table_s), (lens_hbm, lens_s), (fresh_hbm, fresh_ref))
        )
    ]
    for copy in small + loads:
        copy.start()
    row = lax.broadcasted_iota(jnp.int32, (16, head_dim), 0)
    bases, news = [], []
    for copy in small:
        copy.wait()
    for r in range(reqs):
        length = lens_s[r]
        page = table_s[r, length // page_len]
        position = page * page_len + length % page_len
        bases.append(position // 4)
        four = fresh_ref[4 * r : 4 * r + 4, :].astype(F32)
        news.append((row // 4 == position % 4, jnp.concatenate([four, four, four, four], axis=0)))
    stores = []
    for i in range(chunks):
        loads[i].wait()
        for r in range(reqs):

            @pl.when(bases[r] // (chunk // 16) == i)
            def _():
                base = pl.multiple_of(bases[r] * 16, 16)
                hit, tiled = news[r]
                old = kv[pl.ds(base, 16), :].astype(F32)
                kv[pl.ds(base, 16), :] = jnp.where(hit, tiled, old).astype(BF16)

        copy = pltpu.make_async_copy(
            kv.at[pl.ds(i * chunk, chunk)], pool_out.at[pl.ds(i * chunk, chunk)], out_sem.at[i]
        )
        copy.start()
        stores.append(copy)
    for copy in stores:
        copy.wait()


def attend(page_len, table_v, lens_s, q_ref, kv, scores, weight, loads):
    reqs, max_pages = table_v.shape
    head_dim = kv.shape[1]
    page_rows = 4 * page_len
    pages = kv.shape[0] // page_rows
    req_row = lax.broadcasted_iota(jnp.int32, (reqs, page_rows), 0)
    lane = lax.broadcasted_iota(jnp.int32, (reqs, page_rows), 1)
    lens = jnp.zeros((reqs, page_rows), jnp.int32)
    for r in range(reqs):
        lens = jnp.where(req_row == r, lens_s[r], lens)
    last_page = lens // page_len
    rem = lens % page_len
    whole = jnp.zeros((reqs, page_rows), F32)
    partial = jnp.zeros((reqs, page_rows), F32)
    for j in range(max_pages):
        named = lane == table_v[:, j : j + 1]
        whole += jnp.where(named & (last_page > j), 1.0, 0.0)
        partial += jnp.where(named & (last_page == j), 1.0, 0.0)
    seen = (lane // 4) <= rem
    is_key = (lane % 4) < 2
    masks = []
    for head in range(2):
        mine = is_key & ((lane % 2) == head)
        masks.append((jnp.where(mine, 1.0, 0.0), jnp.where(mine & seen, 1.0, 0.0)))
    for p in range(pages):
        full = jnp.broadcast_to(whole[:, p : p + 1], (reqs, page_rows))
        part = jnp.broadcast_to(partial[:, p : p + 1], (reqs, page_rows))
        for head in range(2):
            weight[p, head] = full * masks[head][0] + part * masks[head][1]

    query = q_ref[...].astype(F32)
    heads = query.shape[1] // head_dim
    group = heads // 2
    stacked = jnp.concatenate(
        [query[:, h * head_dim : (h + 1) * head_dim] for h in range(heads)], axis=0
    ).astype(BF16)
    scale = math.log2(math.e) / math.sqrt(head_dim)
    step_rows = 2 * page_rows
    groups = 13
    steps = pages // (2 * groups)

    def rows_of(g, i):
        first = pl.multiple_of((g * steps + i) * step_rows, step_rows)
        return kv[pl.ds(first, step_rows), :]

    def score_group(g, top):
        tops = [top[h * reqs : (h + 1) * reqs, :] for h in range(heads)]
        for i in range(steps):
            s = dot_nt(stacked, rows_of(g, i))
            for half in range(2):
                p = (g * steps + i) * 2 + half
                bias = [jnp.where(weight[p, head] > 0, 0.0, -1e30) for head in range(2)]
                for h in range(heads):
                    piece = s[h * reqs : (h + 1) * reqs, half * page_rows : (half + 1) * page_rows]
                    masked = piece + bias[h // group]
                    scores[p, h * reqs : (h + 1) * reqs, :] = masked
                    tops[h] = jnp.maximum(tops[h], masked)
        return jnp.concatenate(tops, axis=0)

    def value_group(g, carry):
        total, acc = carry
        for i in range(steps):
            parts = []
            for half in range(2):
                p = (g * steps + i) * 2 + half
                w = jnp.concatenate([weight[p, h // group] for h in range(heads)], axis=0)
                e = jnp.exp2((scores[p] - top) * scale) * w
                total += e
                parts.append(pltpu.roll(e, 2, 1).astype(BF16))
            acc += dot_nn(jnp.concatenate(parts, axis=1), rows_of(g, i))
        return total, acc

    for copy in loads:
        copy.wait()
    top = jnp.full((heads * reqs, page_rows), -1e30, F32)
    for g in range(groups):
        top = score_group(g, top)
    top = jnp.max(top, axis=1, keepdims=True)
    carry = (
        jnp.zeros((heads * reqs, page_rows), F32),
        jnp.zeros((heads * reqs, head_dim), F32),
    )
    for g in range(groups):
        carry = value_group(g, carry)
    total, acc = carry
    result = acc / jnp.sum(total, axis=1, keepdims=True)
    return jnp.concatenate(
        [result[h * reqs : (h + 1) * reqs, :] for h in range(heads)], axis=1
    ).astype(BF16)


Z_ORDER = (4, 3, 5, 2, 6, 1, 7)
PLANE_ORDER = (10, 8, 11, 9, 6, 14, 4, 12, 7, 15, 5, 13, 2, 3, 1)


def expert_kernel(
    page_len,
    lens_hbm,
    table_hbm,
    q_hbm,
    hidden_hbm,
    gain_hbm,
    router_hbm,
    ids_hbm,
    pool_hbm,
    ow_hbm,
    gu_hbm,
    down_hbm,
    out_ref,
    stat_ref,
    lens_s,
    table_v,
    q_ref,
    hidden_ref,
    gain_ref,
    ids_ref,
    kv,
    ow,
    scores,
    weight,
    part_ref,
    gu,
    down,
    pbuf,
    router2,
    zbuf,
    zbuf2,
    psend,
    xbuf,
    gu2,
    down2,
    rsend,
    rbuf,
    csend,
    fbuf,
    w_sem,
    kv_sem,
    z_send,
    z_recv,
    p_send,
    p_recv,
    y_sem,
    r_send,
    r_recv,
    c_send,
    c_recv,
    in_sem,
    ow_sem,
    small_sem,
):
    me = lax.axis_index("req")
    k = lax.axis_index("kv")
    core = lax.rem(me, 2)
    xh = lax.rem(lax.div(me, 2), 2)
    y = lax.rem(lax.div(me, 4), 4)
    z = lax.div(me, 16)
    line = y * 2 + xh
    sibling = me + 1 - 2 * core
    rows_y = [y] + [lax.rem(y + d, 4) for d in range(1, 4)]
    rows_x = [xh, 1 - xh]
    rows_k = [k, 1 - k]
    rows_z = [z] + [lax.rem(z + d, 8) for d in range(1, 8)]
    corner = me - line * 2
    offset = me - z * 16

    def plane_peer(i):
        block = rows_y[i // 4] * 2 + rows_x[(i // 2) % 2]
        return corner + block * 2, rows_k[i % 2], block

    def z_peer(d):
        return rows_z[d] * 16 + offset

    experts = router_hbm.shape[0]
    small = [
        pltpu.make_async_copy(source, target, small_sem.at[i])
        for i, (source, target) in enumerate(
            (
                (lens_hbm, lens_s),
                (table_hbm, table_v),
                (q_hbm, q_ref),
                (ids_hbm, ids_ref),
                (hidden_hbm, hidden_ref),
                (gain_hbm, gain_ref),
                (router_hbm, router2.at[pl.ds(0, experts)]),
                (router_hbm, router2.at[pl.ds(experts, experts)]),
            )
        )
    ]
    for copy in small[:3]:
        copy.start()
    chunks = in_sem.shape[0]
    chunk = kv.shape[0] // chunks
    loads = [
        pltpu.make_async_copy(
            pool_hbm.at[pl.ds(i * chunk, chunk)], kv.at[pl.ds(i * chunk, chunk)], in_sem.at[i]
        )
        for i in range(chunks)
    ]
    ow_chunks = ow_sem.shape[0]
    ow_chunk = ow.shape[0] // ow_chunks
    ow_loads = [
        pltpu.make_async_copy(
            ow_hbm.at[pl.ds(i * ow_chunk, ow_chunk)],
            ow.at[pl.ds(i * ow_chunk, ow_chunk)],
            ow_sem.at[i],
        )
        for i in range(ow_chunks)
    ]
    w_loads = [
        pltpu.make_async_copy(gu_hbm.at[0], gu.at[0], w_sem.at[0]),
        pltpu.make_async_copy(gu_hbm.at[1], gu.at[1], w_sem.at[1]),
        pltpu.make_async_copy(down_hbm, down, w_sem.at[2]),
    ]
    for copy in loads + ow_loads + small[3:]:
        copy.start()
    barrier = pltpu.get_barrier_semaphore()
    for i in range(1, 16):
        dev, pk, _ = plane_peer(i)
        pl.semaphore_signal(barrier, inc=1, device_id=(dev, pk), device_id_type=MESH)
    for d in range(1, 8):
        for side in range(2):
            pl.semaphore_signal(barrier, inc=1, device_id=(z_peer(d), side), device_id_type=MESH)
    pl.semaphore_signal(barrier, inc=1, device_id=(sibling, k), device_id_type=MESH)

    for copy in small[:3]:
        copy.wait()
    attended = attend(page_len, table_v, lens_s, q_ref, kv, scores, weight, loads)
    for copy in small[3:]:
        copy.wait()
    for copy in ow_loads:
        copy.wait()
    for copy in w_loads:
        copy.start()
    part_ref[...] = dot_nn(attended, ow[...]).astype(BF16)
    pl.semaphore_wait(barrier, 30)

    swap = pltpu.make_async_remote_copy(
        src_ref=part_ref,
        dst_ref=pbuf,
        send_sem=kv_sem.at[0],
        recv_sem=kv_sem.at[1],
        device_id=(me, 1 - k),
        device_id_type=MESH,
    )
    swap.start()
    lends = []
    for i, (source, target) in enumerate(
        ((gu_hbm.at[0], gu2.at[0]), (gu_hbm.at[1], gu2.at[1]), (down_hbm, down2))
    ):
        copy = pltpu.make_async_remote_copy(
            src_ref=source,
            dst_ref=target,
            send_sem=y_sem.at[2 * i],
            recv_sem=y_sem.at[2 * i + 1],
            device_id=(sibling, k),
            device_id_type=MESH,
        )
        copy.start()
        lends.append(copy)
    tokens, width = hidden_ref.shape
    half = width // 2
    chosen_count = ids_ref.shape[1]
    lane = lax.broadcasted_iota(jnp.int32, (tokens, 2 * experts), 1)
    chosen = jnp.zeros((tokens, 2 * experts), F32)
    for j in range(chosen_count):
        chosen += jnp.where(lane % experts == ids_ref[:, j : j + 1], 1.0, 0.0)
    swap.wait()
    projected = part_ref[...].astype(F32) + pbuf[...].astype(F32)
    mixed = (hidden_ref[...].astype(F32) + projected).astype(BF16).astype(F32)
    norms = jnp.sqrt(jnp.sum(mixed * mixed, axis=1, keepdims=True) / width + 1e-06)
    normed = (mixed / norms * gain_ref[...].astype(F32).reshape(1, width)).astype(BF16)
    logits = dot_nt(normed, router2[...])
    stat_ref[...] = jnp.where(
        lane == 0, norms, jnp.max(logits, axis=1, keepdims=True)
    )
    raised = jnp.where(chosen > 0, jnp.exp(logits), 0.0)
    gates = raised / jnp.sum(jnp.where(lane < experts, raised, 0.0), axis=1, keepdims=True)
    high = gates.astype(BF16).astype(F32)
    meta = jnp.where(lane < experts, jnp.where(chosen > 0, high, -1.0), gates - high)

    normed32 = normed.astype(F32)
    own_half = jnp.where(k == 0, normed32[:, :half], normed32[:, half:])
    part_width = half // 2
    zbuf[z] = jnp.concatenate([own_half[:, :part_width], meta], axis=1).astype(BF16)
    zbuf2[z] = own_half[:, part_width:].astype(BF16)
    z_copies = []
    for q, buffer in enumerate((zbuf, zbuf2)):
        for d in Z_ORDER:
            copy = pltpu.make_async_remote_copy(
                src_ref=buffer.at[z],
                dst_ref=buffer.at[z],
                send_sem=z_send.at[8 * q + d],
                recv_sem=z_recv.at[8 * q + d],
                device_id=(z_peer(d), k),
                device_id_type=MESH,
            )
            copy.start()
            z_copies.append(copy)

    count = 8 * tokens
    slots = 128
    row = lax.broadcasted_iota(jnp.int32, (slots, 2 * experts), 0)
    col = lax.broadcasted_iota(jnp.int32, (slots, 2 * experts), 1)
    pick_high = jnp.where(col == 8 * z + row // 16, 1.0, 0.0).astype(BF16)
    pick_low = jnp.where(col == experts + 8 * z + row // 16, 1.0, 0.0).astype(BF16)
    row = lax.broadcasted_iota(jnp.int32, (count, count), 0)
    col = lax.broadcasted_iota(jnp.int32, (count, count), 1)
    same = row // tokens == col // tokens
    before = jnp.where(same & (row < col), 1.0, 0.0).astype(BF16)
    after = jnp.where(same & (col < row), 1.0, 0.0).astype(BF16)

    for copy in z_copies[:7]:
        copy.wait_recv()
    gathered = zbuf[...].astype(F32).reshape(count, part_width + 2 * experts)
    metas = gathered[:, part_width:].astype(BF16)
    row = lax.broadcasted_iota(jnp.int32, (slots, count), 0)
    col = lax.broadcasted_iota(jnp.int32, (slots, count), 1)
    taken = jnp.where(dot_nt(pick_high, metas) >= 0, 1.0, 0.0)
    rank = dot_nn(taken.astype(BF16), before)
    hit = (taken > 0) & (col // tokens == (row // 2) % 8) & (rank == (row % 2).astype(F32))
    dispatch = jnp.where(hit, 1.0, 0.0).astype(BF16)
    p_copies = {}
    for q in range(2):
        if q == 0:
            states = gathered[:, :part_width].astype(BF16)
        else:
            for copy in z_copies[7:]:
                copy.wait_recv()
            states = zbuf2[...].astype(F32).reshape(count, part_width).astype(BF16)
        psend[q] = dot_nn(dispatch, states).reshape(8, 16, part_width).astype(BF16)
        for i in PLANE_ORDER:
            dev, pk, block = plane_peer(i)
            copy = pltpu.make_async_remote_copy(
                src_ref=psend.at[q, block],
                dst_ref=xbuf.at[k, q, line],
                send_sem=p_send.at[16 * q + i],
                recv_sem=p_recv.at[16 * q + i],
                device_id=(dev, pk),
                device_id_type=MESH,
            )
            copy.start()
            p_copies[16 * q + i] = copy
        xbuf[k, q, line] = psend[q, line]

    row = lax.broadcasted_iota(jnp.int32, (count, slots), 0)
    col = lax.broadcasted_iota(jnp.int32, (count, slots), 1)
    gate_high = dot_nt(metas, pick_high)
    gate_low = dot_nt(metas, pick_low)
    taken = jnp.where(gate_high >= 0, 1.0, 0.0)
    rank = dot_nn(after, taken.astype(BF16))
    hit = (taken > 0) & (row // tokens == (col // 2) % 8) & (rank == (col % 2).astype(F32))
    combine_high = jnp.where(hit, gate_high, 0.0).astype(BF16)
    combine_low = jnp.where(hit, gate_low, 0.0).astype(BF16)

    for copy in w_loads:
        copy.wait()
    sums = [jnp.zeros((slots, down.shape[0]), F32) for _ in range(4)]
    for q in range(2):
        for i in PLANE_ORDER:
            p_copies[16 * q + i].wait_recv()
        blocks = [
            xbuf[part, q].astype(F32).reshape(slots, part_width).astype(BF16) for part in range(2)
        ]
        for j, weights in enumerate((gu, gu2)):
            if q == 0 and j == 1:
                for copy in lends[:2]:
                    copy.wait_recv()
            for part in range(2):
                first = part * half + q * part_width
                for side in range(2):
                    sums[2 * j + side] += dot_nt(
                        blocks[part], weights[side, :, first : first + part_width]
                    )
    lends[2].wait_recv()
    acts = []
    for j in range(2):
        gate, up = sums[2 * j], sums[2 * j + 1]
        acts.append((gate / (1.0 + jnp.exp(-gate)) * up).astype(BF16))
    r_copies = []
    for q in range(2):
        for part in range(2):
            first = part * half + q * part_width
            last = first + part_width
            both = dot_nn(acts[0], down[:, first:last]) + dot_nn(acts[1], down2[:, first:last])
            rsend[q, part] = both.reshape(8, 16, part_width).astype(BF16)
        for i in PLANE_ORDER:
            dev, pk, block = plane_peer(i)
            copy = pltpu.make_async_remote_copy(
                src_ref=rsend.at[q, pk, block],
                dst_ref=rbuf.at[q, k, line],
                send_sem=r_send.at[16 * q + i],
                recv_sem=r_recv.at[16 * q + i],
                device_id=(dev, pk),
                device_id_type=MESH,
            )
            copy.start()
            r_copies.append(copy)
        rbuf[q, k, line] = rsend[q, k, line]
    c_copies = []
    for q in range(2):
        for copy in r_copies[15 * q : 15 * q + 15]:
            copy.wait_recv()
        routed = jnp.zeros((count, part_width), F32)
        for side in range(2):
            block = rbuf[q, side].astype(F32).reshape(slots, part_width).astype(BF16)
            routed += dot_nn(combine_high, block) + dot_nn(combine_low, block)
        csend[q] = routed.reshape(8, tokens, part_width).astype(BF16)
        for j, d in enumerate(Z_ORDER + (0,)):
            for flip in (1, 0):
                if d + flip > 0:
                    copy = pltpu.make_async_remote_copy(
                        src_ref=csend.at[q, rows_z[d]],
                        dst_ref=fbuf.at[q, k, z],
                        send_sem=c_send.at[16 * q + 2 * j + flip],
                        recv_sem=c_recv.at[16 * q + 2 * j + flip],
                        device_id=(z_peer(d), rows_k[flip]),
                        device_id_type=MESH,
                    )
                    copy.start()
                    c_copies.append(copy)
        fbuf[q, k, z] = csend[q, z]
    for q in range(2):
        for copy in c_copies[15 * q : 15 * q + 15]:
            copy.wait_recv()
        for side in range(2):
            total = jnp.sum(fbuf[q, side].astype(F32), axis=0)
            first = side * half + q * part_width
            last = first + part_width
            out_ref[:, first:last] = (mixed[:, first:last] + total).astype(BF16)
    for copy in lends + z_copies + list(p_copies.values()) + r_copies + c_copies:
        copy.wait_send()


def finish_kernel(hidden_ref, stat_ref, out_ref, norm_ref, logit_ref):
    out_ref[...] = hidden_ref[...]
    stats = stat_ref[...]
    row = lax.broadcasted_iota(jnp.int32, stats.shape, 0)
    col = lax.broadcasted_iota(jnp.int32, stats.shape, 1)
    for target, lane in ((norm_ref, 0), (logit_ref, 1)):
        column = jnp.broadcast_to(stats[:, lane : lane + 1], stats.shape)
        line = jnp.sum(jnp.where(row == col, column, 0.0), axis=0)
        target[...] = line[: target.shape[0]]


def to_rows(array):
    lead = math.prod(array.shape[:-2])
    head_dim = array.shape[-1] // 2
    split = array.reshape(lead, array.shape[-2], 2, head_dim)
    return split.transpose(0, 2, 1, 3).reshape(-1, head_dim)


def body(
    hidden,
    queries,
    fresh_key_value,
    kv_pool,
    page_table,
    lengths,
    out_weight,
    norm_gain,
    router_weight,
    expert_ids,
    expert_gate_up,
    expert_down,
):
    tokens, width = hidden.shape
    half = width // 2
    pages, page_len, kv_heads, pair = kv_pool.shape
    head_dim = pair // 2
    pool_rows = to_rows(kv_pool)
    fresh_rows = to_rows(fresh_key_value)
    rows = pool_rows.shape[0]
    heads = queries.shape[1] // head_dim
    page_rows = rows // pages
    vmem = pl.BlockSpec(memory_space=pltpu.VMEM)
    hbm = pl.BlockSpec(memory_space=pltpu.HBM)
    pool_new = pl.pallas_call(
        functools.partial(pool_kernel, page_len),
        out_shape=jax.ShapeDtypeStruct(pool_rows.shape, BF16),
        in_specs=[hbm, hbm, hbm, hbm],
        out_specs=hbm,
        scratch_shapes=[
            pltpu.SMEM(page_table.shape, jnp.int32),
            pltpu.SMEM(lengths.shape, jnp.int32),
            pltpu.VMEM(fresh_rows.shape, BF16),
            pltpu.VMEM(pool_rows.shape, BF16),
            pltpu.SemaphoreType.DMA((8,)),
            pltpu.SemaphoreType.DMA((8,)),
            pltpu.SemaphoreType.DMA((3,)),
        ],
    )(page_table, lengths, fresh_rows, pool_rows)
    updated_pool = (
        pool_new.reshape(pages * page_len, 2, kv_heads, head_dim)
        .transpose(0, 2, 1, 3)
        .reshape(kv_pool.shape)
    )
    gate_up = expert_gate_up[0]
    down = expert_down[0]
    experts = router_weight.shape[0]
    dma = pltpu.SemaphoreType.DMA
    out_raw, stats = pl.pallas_call(
        functools.partial(expert_kernel, page_len),
        out_shape=(
            jax.ShapeDtypeStruct((tokens, width), BF16),
            jax.ShapeDtypeStruct((tokens, 2 * experts), F32),
        ),
        in_specs=[hbm] * 11,
        out_specs=(vmem, vmem),
        scratch_shapes=[
            pltpu.SMEM(lengths.shape, jnp.int32),
            pltpu.VMEM(page_table.shape, jnp.int32),
            pltpu.VMEM(queries.shape, BF16),
            pltpu.VMEM(hidden.shape, BF16),
            pltpu.VMEM(norm_gain.shape, BF16),
            pltpu.VMEM(expert_ids.shape, jnp.int32),
            pltpu.VMEM(pool_rows.shape, BF16),
            pltpu.VMEM(out_weight.shape, BF16),
            pltpu.VMEM((pages, heads * tokens, page_rows), F32),
            pltpu.VMEM((pages, 2, tokens, page_rows), F32),
            pltpu.VMEM((tokens, width), BF16),
            pltpu.VMEM(gate_up.shape, BF16),
            pltpu.VMEM(down.shape, BF16),
            pltpu.VMEM((tokens, width), BF16),
            pltpu.VMEM((2 * experts, width), BF16),
            pltpu.VMEM((8, tokens, half // 2 + 2 * experts), BF16),
            pltpu.VMEM((8, tokens, half // 2), BF16),
            pltpu.VMEM((2, 8, 16, half // 2), BF16),
            pltpu.VMEM((2, 2, 8, 16, half // 2), BF16),
            pltpu.VMEM(gate_up.shape, BF16),
            pltpu.VMEM(down.shape, BF16),
            pltpu.VMEM((2, 2, 8, 16, half // 2), BF16),
            pltpu.VMEM((2, 2, 8, 16, half // 2), BF16),
            pltpu.VMEM((2, 8, tokens, half // 2), BF16),
            pltpu.VMEM((2, 2, 8, tokens, half // 2), BF16),
            dma((3,)),
            dma((2,)),
            dma((16,)),
            dma((16,)),
            dma((32,)),
            dma((32,)),
            dma((6,)),
            dma((32,)),
            dma((32,)),
            dma((32,)),
            dma((32,)),
            dma((13,)),
            dma((4,)),
            dma((8,)),
        ],
        compiler_params=pltpu.CompilerParams(collective_id=0, has_side_effects=True),
    )(
        lengths,
        page_table,
        queries,
        hidden,
        norm_gain,
        router_weight,
        expert_ids,
        pool_new,
        out_weight,
        gate_up,
        down,
    )
    out_hidden, norms, max_logit = pl.pallas_call(
        finish_kernel,
        out_shape=(
            jax.ShapeDtypeStruct((tokens, width), BF16),
            jax.ShapeDtypeStruct((tokens,), F32),
            jax.ShapeDtypeStruct((tokens,), F32),
        ),
        in_specs=[vmem, vmem],
        out_specs=(vmem, vmem, vmem),
    )(out_raw, stats)
    return (out_hidden, updated_pool, norms, max_logit)


def solution(mesh):
    in_specs = (
        P("req", None),
        P("req", "kv"),
        P("req", "kv", None),
        P("req", None, "kv", None),
        P("req", None),
        P("req"),
        P("kv", None),
        P(),
        P(),
        P("req", None),
        P("req", None, "kv", None),
        P("req", "kv", None),
    )
    out_specs = (P("req", None), P("req", None, "kv", None), P("req"), P("req"))
    return jax.shard_map(body, mesh=mesh, in_specs=in_specs, out_specs=out_specs, check_vma=False)
```
